128 devices in a mesh: frame: 2 (over x_hi), height: 8 (over z, core), width: 8 (over y, x_lo).
Axes of the slice: x: 4 (x_hi: 2, x_lo: 2; x = x_hi * 2 + x_lo), y: 4, z: 4, core: 2. Of those that a mesh axis runs over, the one named last changes fastest.
Arguments:
- activations: bfloat16 [8, 128, 256, 256], P('frame', 'height', 'width'), may hold values from -6 to 6
- out_grad: bfloat16 [8, 128, 256, 256], P('frame', 'height', 'width'), may hold values from -40 to 40
- kernel: bfloat16 [6912, 256], P(('frame', 'height', 'width')), may hold values from -5 to 5
- damping: float32 [], replicated, may hold values from 0.02 to 0.2
Outputs:
- input_grad: bfloat16 [8, 128, 256, 256], P('frame', 'height', 'width')
- new_kernel: bfloat16 [6912, 256], replicated
The draws below stay inside these ranges and needn't reach their ends.
All inputs are finite; a program needn't handle non-finite values.
Results may differ from the reference program's by a relative error of at most 0.001.
Values may be sent and summed in bfloat16 or wider, within the bound.
A program may use at most 192 MiB of HBM per device.

```python
import math
import jax
import jax.numpy as jnp
from jax import lax

C = 256
ITERS = 12
NF = 8
NH = 128
NW = 256
KROWS = 6912


def draw_out_grad(key, part):
    first, second = jax.random.split(jax.random.fold_in(key, 7))
    scales = jnp.exp(jax.random.uniform(first, (C,), jnp.float32, math.log(0.1), math.log(10.0)))
    base = jnp.clip(jax.random.normal(second, (NF, NH, NW, C), jnp.float32), -4.0, 4.0)
    return (base * scales).astype(jnp.bfloat16)


def shard_levels(rng, dims, cuts, smallest, top_value):
    def one(position, blocks):
        heights = jax.random.uniform(jax.random.fold_in(jax.random.fold_in(rng, 6), position), (blocks,), jnp.float32, smallest / len(cuts), top_value / len(cuts))
        return jnp.repeat(jnp.exp(heights), dims[position] // blocks).reshape((-1,) + (1,) * (len(dims) - position - 1))

    loudness = one(*cuts[0])
    for cut in cuts[1:]:
        loudness = loudness * one(*cut)
    return loudness


def normal_values(own_key, extent, deviation, bound, shards=(), kind=jnp.bfloat16):
    level = shard_levels(own_key, extent, shards, -0.22, 0.18) if shards else 1.0
    drawn = jax.random.normal(own_key, extent, jnp.float32) * deviation * level
    return jnp.minimum(jnp.maximum(drawn, -bound), bound).astype(kind)


def setup_inputs(seed: int = 0) -> dict:
    key_of = jax.random.split(jax.random.key(seed), 5)
    return {
        "activations": normal_values(key_of[0], (NF, NH, NW, C), 1.0, 6.0, ((0, 2), (1, 8), (2, 8))),
        "out_grad": draw_out_grad(jax.random.fold_in(key_of[4], 71), 0),
        "kernel": normal_values(key_of[2], (KROWS, C), 1.0, 5.0, ((0, 128),)),
        "damping": jnp.clip(jnp.exp(jax.random.uniform(key_of[3], (), jnp.float32, math.log(0.02), math.log(0.2))), 0.02, 0.2),
    }


def newton_root(gram, damping):
    order = gram.shape[0]
    identity = jnp.eye(order, dtype=jnp.float32)
    factor = gram + damping * (jnp.trace(gram) / order) * identity
    start_scale = 2.5 / jnp.sqrt(jnp.sum(factor * factor))
    inverse_root = jnp.sqrt(jnp.sqrt(start_scale)) * identity
    matrix = start_scale * factor
    for step in range(ITERS):
        middle = (5.0 * identity - matrix) / 4.0
        inverse_root = jnp.dot(inverse_root, middle, precision=lax.Precision.HIGHEST)
        square = jnp.dot(middle, middle, precision=lax.Precision.HIGHEST)
        matrix = jnp.dot(square, jnp.dot(square, matrix, precision=lax.Precision.HIGHEST), precision=lax.Precision.HIGHEST)
    return inverse_root

def frame_padded(volume, index):
    frames = volume.shape[0]
    safe = jnp.clip(index, 0, frames - 1).astype(jnp.int32)
    piece = lax.dynamic_index_in_dim(volume, safe, 0, keepdims=False)
    valid = jnp.logical_and(index >= 0, index < frames)
    piece = jnp.where(valid, piece, jnp.zeros_like(piece))
    return jnp.pad(piece, ((1, 1), (1, 1), (0, 0)))

def reference(activations, out_grad, kernel, damping):
    frames, height, width, chans = activations.shape
    count = height * width
    krows = kernel.shape[0]

    def one_frame(carry, index):
        own_grad = lax.dynamic_index_in_dim(out_grad, index.astype(jnp.int32), 0, keepdims=False).reshape(count, chans)
        pieces = []
        total = jnp.zeros((count, chans), jnp.float32)
        for tap_f in range(3):
            slab_in = frame_padded(activations, index + tap_f - 1)
            slab_grad = frame_padded(out_grad, index + 1 - tap_f)
            for tap_h in range(3):
                for tap_w in range(3):
                    tap = 9 * tap_f + 3 * tap_h + tap_w
                    shifted = slab_in[tap_h:tap_h + height, tap_w:tap_w + width].reshape(count, chans)
                    pieces.append(lax.dot_general(shifted, own_grad, (((0,), (0,)), ((), ())), preferred_element_type=jnp.float32))
                    back = slab_grad[2 - tap_h:2 - tap_h + height, 2 - tap_w:2 - tap_w + width].reshape(count, chans)
                    total = total + jnp.dot(back, kernel[tap * chans:(tap + 1) * chans], preferred_element_type=jnp.float32)
        frame_grad = (total / jnp.sqrt(jnp.float32(krows))).astype(jnp.bfloat16).reshape(height, width, chans)
        return (carry + jnp.concatenate(pieces, 0), frame_grad)
    start = jnp.zeros((krows, chans), jnp.float32)
    kernel_grad, input_grad = lax.scan(one_frame, start, jnp.arange(frames, dtype=jnp.int32))
    gram = lax.dot_general(kernel_grad, kernel_grad, (((0,), (0,)), ((), ())), precision=lax.Precision.HIGHEST)
    inverse_root = newton_root(gram, damping)
    direction = jnp.dot(kernel_grad, inverse_root, precision=lax.Precision.HIGHEST)
    size = jnp.sqrt(jnp.mean(direction * direction) + 1e-06)
    new_kernel = (kernel.astype(jnp.float32) - 0.5 * direction / size).astype(jnp.bfloat16)
    return (input_grad, new_kernel)
```

```python
import functools

import jax
import jax.numpy as jnp
from jax import lax
from jax.experimental import pallas as pl
from jax.experimental.pallas import tpu as pltpu
from jax.sharding import PartitionSpec as P

MESH = pl.DeviceIdType.MESH
ITERS = 12
VMEM = pltpu.VMEM
BF = jnp.bfloat16
F32 = jnp.float32
LIMIT = 64000 * 1024
ORDERS = (("x", "y", "z"), ("y", "z", "x"), ("z", "x", "y"))
CUTS = ((0, 2), (2, 4), (4, 7))


def place():
    f, h, w = lax.axis_index("frame"), lax.axis_index("height"), lax.axis_index("width")
    return {"x": 2 * f + w % 2, "y": w // 2, "z": h // 2, "c": h % 2}


def device(at):
    return (at["x"] // 2, 2 * at["z"] + at["c"], 2 * at["y"] + at["x"] % 2)


def along(at, axis, k):
    moved = dict(at)
    moved[axis] = (at[axis] + k) % 4
    return device(moved)


def other_core(at):
    moved = dict(at)
    moved["c"] = 1 - at["c"]
    return device(moved)


def meet(partners):
    barrier = pltpu.get_barrier_semaphore()
    for partner in partners:
        pl.semaphore_signal(barrier, inc=1, device_id=partner, device_id_type=MESH)
    pl.semaphore_wait(barrier, len(partners))


def send(src, dst, sems, index, to):
    copy = pltpu.make_async_remote_copy(
        src_ref=src,
        dst_ref=dst,
        send_sem=sems[0].at[index],
        recv_sem=sems[1].at[index],
        device_id=to,
        device_id_type=MESH,
    )
    copy.start()
    return copy


def halo_kernel(g, own, gc, lc, rc, k0, k1, k2, edge, hsem, hrsem, ksem, krsem, lsem):
    at = place()
    f, h, w = lax.axis_index("frame"), lax.axis_index("height"), lax.axis_index("width")
    up, down = (f, (h + 7) % 8, w), (f, (h + 1) % 8, w)
    left, right = (f, h, (w + 7) % 8), (f, h, (w + 1) % 8)
    across = (1 - f, h, w)
    parts = (k0, k1, k2)
    hs, ks = (hsem, hrsem), (ksem, krsem)
    core = at["c"]
    index = [at[o[2]] * 16 + at[o[1]] * 4 + at[o[0]] for o in ORDERS]

    locals_ = [pltpu.make_async_copy(g, gc.at[0:4, 1:17], lsem.at[0])]
    for p, (lo, hi) in enumerate(CUTS):
        locals_.append(
            pltpu.make_async_copy(own.at[lo:hi], parts[p].at[core, index[p]], lsem.at[1 + p])
        )
    for copy in locals_:
        copy.start()
    meet(
        [up, down, left, right, across, other_core(at)]
        + [along(at, axis, k) for axis in "xyz" for k in (1, 2, 3)]
    )
    edge_frame = 3 * (1 - f)
    rows = [
        send(g.at[:, 0:1], gc.at[0:4, 17:18], hs, 0, up),
        send(g.at[:, 15:16], gc.at[0:4, 0:1], hs, 1, down),
    ]
    face = send(g.at[edge_frame], gc.at[4, 1:17], hs, 2, across)
    one = [
        send(own.at[lo:hi], parts[p].at[core, index[p]], ks, 9 * p + k - 1, along(at, ORDERS[p][0], k))
        for p, (lo, hi) in enumerate(CUTS)
        for k in (1, 2, 3)
    ]
    locals_[0].wait()
    for copy in rows:
        copy.wait_recv()
    face_rows = [
        send(gc.at[edge_frame, 0:1], gc.at[4, 0:1], hs, 3, across),
        send(gc.at[edge_frame, 17:18], gc.at[4, 17:18], hs, 4, across),
    ]
    line = lax.broadcasted_iota(jnp.int32, (64, 576), 0)
    spot = lax.broadcasted_iota(jnp.int32, (64, 576), 1)
    want = jnp.where(line < 32, line * 32 + 31, (line - 32) * 32)
    pick = jnp.where(spot == want, 1.0, 0.0).astype(BF)
    for frame in range(4):
        block = gc[frame].reshape(576, 256)
        cut = jnp.dot(pick, block, preferred_element_type=F32).astype(BF)
        edge[0, frame] = cut[:32]
        edge[1, frame] = cut[32:]
    columns = [
        send(edge.at[0], lc.at[0:4], hs, 5, right),
        send(edge.at[1], rc.at[0:4], hs, 6, left),
    ]
    for copy in locals_[1:]:
        copy.wait()
    two = []
    for p in range(3):
        for copy in one[3 * p : 3 * p + 3]:
            copy.wait_recv()
        held = parts[p].at[core, pl.ds(at[ORDERS[p][2]] * 16 + at[ORDERS[p][1]] * 4, 4)]
        two += [
            send(held, held, ks, 9 * p + 3 + k - 1, along(at, ORDERS[p][1], k)) for k in (1, 2, 3)
        ]
    for copy in columns:
        copy.wait_recv()
    face_columns = [
        send(lc.at[edge_frame], lc.at[4], hs, 7, across),
        send(rc.at[edge_frame], rc.at[4], hs, 8, across),
    ]
    three = []
    for p in range(3):
        for copy in two[3 * p : 3 * p + 3]:
            copy.wait_recv()
        held = parts[p].at[core, pl.ds(at[ORDERS[p][2]] * 16, 16)]
        three += [
            send(held, held, ks, 9 * p + 6 + k - 1, along(at, ORDERS[p][2], k)) for k in (1, 2, 3)
        ]
    pair = []
    for p in range(3):
        for copy in three[3 * p : 3 * p + 3]:
            copy.wait_recv()
        pair.append(send(parts[p].at[core], parts[p].at[core], ks, 27 + p, other_core(at)))
    for copy in [face] + face_rows + face_columns + pair:
        copy.wait_recv()
    for copy in rows + [face] + face_rows + columns + face_columns + one + two + three + pair:
        copy.wait_send()


def halo(g, own):
    return pl.pallas_call(
        halo_kernel,
        out_shape=(
            jax.ShapeDtypeStruct((5, 18, 32, 256), BF),
            jax.ShapeDtypeStruct((5, 32, 256), BF),
            jax.ShapeDtypeStruct((5, 32, 256), BF),
        )
        + tuple(jax.ShapeDtypeStruct((2, 64, hi - lo, 8, 256), BF) for lo, hi in CUTS),
        in_specs=[pl.BlockSpec(memory_space=pl.ANY)] * 2,
        out_specs=[pl.BlockSpec(memory_space=VMEM)] * 6,
        scratch_shapes=[
            VMEM((2, 4, 32, 256), BF),
            pltpu.SemaphoreType.DMA((9,)),
            pltpu.SemaphoreType.DMA((9,)),
            pltpu.SemaphoreType.DMA((30,)),
            pltpu.SemaphoreType.DMA((30,)),
            pltpu.SemaphoreType.DMA((4,)),
        ],
        compiler_params=pltpu.CompilerParams(
            collective_id=0, has_side_effects=True, vmem_limit_bytes=LIMIT
        ),
        name="halo",
    )(g, own)


def conv_kernel(act, gc, lc, rc, k0, k1, k2, kg, ig, kal, gs, lf, rf, act_t, mix):
    f, h, w = lax.axis_index("frame"), lax.axis_index("height"), lax.axis_index("width")
    lf[...] = jnp.where(w == 0, 0.0, lc[...].astype(F32))
    rf[...] = jnp.where(w == 7, 0.0, rc[...].astype(F32))
    empty = 5 * f
    sub = lax.broadcasted_iota(jnp.int32, (32, 256), 0)

    def build(r, carry):
        frame, row = r // 18, r % 18
        slot = jnp.where(frame == 4, 5 * (1 - f), frame + 1)
        off = jnp.logical_or(
            jnp.logical_and(row == 0, h == 0), jnp.logical_and(row == 17, h == 7)
        )
        keep = jnp.where(off, 0.0, 1.0)
        x = gc[frame, row].astype(F32) * keep
        before = lf[frame, pl.ds(row, 1), :] * keep
        after = rf[frame, pl.ds(row, 1), :] * keep
        gs[1, slot, row] = x.astype(BF)
        gs[0, slot, row] = jnp.where(sub == 31, after, pltpu.roll(x, 31, 0)).astype(BF)
        gs[2, slot, row] = jnp.where(sub == 0, before, pltpu.roll(x, 1, 0)).astype(BF)
        return carry

    lax.fori_loop(0, 90, build, 0)

    def clear(r, carry):
        for c in range(3):
            gs[c, empty, r] = jnp.zeros((32, 256), BF)
        return carry

    lax.fori_loop(0, 18, clear, 0)

    def align(r, carry):
        x_hi, z, c = r // 8, (r // 2) % 4, r % 2
        for col in range(8):
            spot = {"x": 2 * x_hi + col % 2, "y": col // 2, "z": z}
            for p, (part, (lo, hi)) in enumerate(zip((k0, k1, k2), CUTS)):
                o = ORDERS[p]
                block = part[c, spot[o[2]] * 16 + spot[o[1]] * 4 + spot[o[0]]].astype(F32)
                for j in range(lo, hi):
                    size = 6 if j == 6 else 8
                    mix[54 * col + 8 * j : 54 * col + 8 * j + size] = block[j - lo][:size]
        kal[pl.ds(pl.multiple_of(r * 432, 432), 432), :] = mix[...].astype(BF)
        return carry

    lax.fori_loop(0, 16, align, 0)

    for n in range(8):
        block = act[256 * n : 256 * n + 256, :].astype(F32)
        act_t[:, 256 * n : 256 * n + 256] = block.T.astype(BF)

    def weight(t, carry):
        a, b, c = t // 9, (t // 3) % 3, t % 3
        s = gs[c, pl.ds(2 - a, 4), pl.ds(2 - b, 16)].reshape(2048, 256)
        kg[t] = jnp.dot(act_t[...], s, preferred_element_type=F32)
        return carry

    lax.fori_loop(0, 27, weight, 0)

    def data(q, carry):
        taps = [
            gs[t % 3, q + 2 - t // 9, pl.ds(2 - (t // 3) % 3, 16)].reshape(512, 256)
            for t in range(27)
        ]
        total = jnp.dot(jnp.concatenate(taps, 1), kal[...], preferred_element_type=F32)
        ig[pl.ds(pl.multiple_of(q * 512, 512), 512), :] = (
            total / jnp.sqrt(jnp.float32(6912))
        ).astype(BF)
        return carry

    lax.fori_loop(0, 4, data, 0)


def conv(act, gc, lc, rc, k0, k1, k2):
    return pl.pallas_call(
        conv_kernel,
        out_shape=(
            jax.ShapeDtypeStruct((27, 256, 256), F32),
            jax.ShapeDtypeStruct((2048, 256), BF),
            jax.ShapeDtypeStruct((6912, 256), BF),
        ),
        in_specs=[pl.BlockSpec(memory_space=VMEM)] * 7,
        out_specs=[pl.BlockSpec(memory_space=VMEM)] * 3,
        scratch_shapes=[
            VMEM((3, 6, 18, 32, 256), BF),
            VMEM((5, 32, 256), F32),
            VMEM((5, 32, 256), F32),
            VMEM((256, 2048), BF),
            VMEM((432, 256), F32),
        ],
        compiler_params=pltpu.CompilerParams(vmem_limit_bytes=LIMIT),
        name="conv",
    )(act, gc, lc, rc, k0, k1, k2)


def sum_kernel(kg, f0, f1, f2, r0, s1, ra, s2, rb, s3, rc, sems, rsems):
    at = place()
    core = at["c"]
    partner = other_core(at)
    meet([partner] + [along(at, axis, k) for axis in "xyz" for k in (1, 2, 3)])
    full = (f0, f1, f2)
    pairs = (sems, rsems)
    waits = []

    def go(src, dst, index, to):
        copy = send(src, dst, pairs, index, to)
        waits.append(copy)
        return copy

    zero = [
        go(kg.at[pl.ds(9 * p, 9), pl.ds(1 - core, 1)], r0.at[pl.ds(9 * p, 9)], p, partner)
        for p in range(3)
    ]
    one = []
    for p in range(3):
        zero[p].wait_recv()

        def add(t, carry, p=p):
            s1[9 * p + t] = kg[9 * p + t, core] + r0[9 * p + t, 0]
            return carry

        lax.fori_loop(0, 9, add, 0)
        axis = ORDERS[p][0]
        for k in (1, 2, 3):
            there = (at[axis] + k) % 4
            one.append(
                go(
                    s1.at[pl.ds(9 * p, 9), pl.ds(there, 1)],
                    ra.at[p, k - 1],
                    3 + 3 * p + k - 1,
                    along(at, axis, k),
                )
            )
    two = []
    for p in range(3):
        for copy in one[3 * p : 3 * p + 3]:
            copy.wait_recv()
        mine = at[ORDERS[p][0]]

        def add(t, carry, p=p, mine=mine):
            s2[p, t] = (s1[9 * p + t, mine] + ra[p, 1, t, 0]) + (ra[p, 0, t, 0] + ra[p, 2, t, 0])
            return carry

        lax.fori_loop(0, 9, add, 0)
        axis = ORDERS[p][1]
        for k in (1, 2, 3):
            there = (at[axis] + k) % 4
            two.append(
                go(
                    s2.at[p, :, pl.ds(there, 1)],
                    rb.at[p, k - 1],
                    12 + 3 * p + k - 1,
                    along(at, axis, k),
                )
            )
    three = []
    for p in range(3):
        for copy in two[3 * p : 3 * p + 3]:
            copy.wait_recv()
        mine = at[ORDERS[p][1]]

        def add(t, carry, p=p, mine=mine):
            s3[p, t] = (s2[p, t, mine] + rb[p, 1, t, 0]) + (rb[p, 0, t, 0] + rb[p, 2, t, 0])
            return carry

        lax.fori_loop(0, 9, add, 0)
        for k in (1, 2, 3):
            three.append(
                go(s3.at[p], rc.at[p, k - 1], 21 + 3 * p + k - 1, along(at, ORDERS[p][2], k))
            )
    four = []
    for p in range(3):
        for copy in three[3 * p : 3 * p + 3]:
            copy.wait_recv()
        spot = at[ORDERS[p][0]] * 4 + at[ORDERS[p][1]]

        def add(t, carry, p=p, spot=spot):
            full[p][core, spot, t] = (s3[p, t] + rc[p, 1, t]) + (rc[p, 0, t] + rc[p, 2, t])
            return carry

        lax.fori_loop(0, 9, add, 0)
        held = full[p].at[core, pl.ds(spot, 1)]
        for k in (1, 2, 3):
            four.append(go(held, held, 30 + 3 * p + k - 1, along(at, ORDERS[p][1], k)))
    five = []
    for p in range(3):
        for copy in four[3 * p : 3 * p + 3]:
            copy.wait_recv()
        held = full[p].at[core, pl.ds(at[ORDERS[p][0]] * 4, 4)]
        for k in (1, 2, 3):
            five.append(go(held, held, 39 + 3 * p + k - 1, along(at, ORDERS[p][0], k)))
    six = []
    for p in range(3):
        for copy in five[3 * p : 3 * p + 3]:
            copy.wait_recv()
        six.append(go(full[p].at[core], full[p].at[core], 48 + p, partner))
    for copy in six:
        copy.wait_recv()
    for copy in waits:
        copy.wait_send()


def summed(kg):
    return pl.pallas_call(
        sum_kernel,
        out_shape=(jax.ShapeDtypeStruct((2, 16, 9, 8, 256), F32),) * 3,
        in_specs=[pl.BlockSpec(memory_space=VMEM)],
        out_specs=[pl.BlockSpec(memory_space=VMEM)] * 3,
        scratch_shapes=[
            VMEM((27, 1, 4, 4, 8, 256), F32),
            VMEM((27, 4, 4, 8, 256), F32),
            VMEM((3, 3, 9, 1, 4, 8, 256), F32),
            VMEM((3, 9, 4, 8, 256), F32),
            VMEM((3, 3, 9, 1, 8, 256), F32),
            VMEM((3, 9, 8, 256), F32),
            VMEM((3, 3, 9, 8, 256), F32),
            pltpu.SemaphoreType.DMA((51,)),
            pltpu.SemaphoreType.DMA((51,)),
        ],
        compiler_params=pltpu.CompilerParams(
            collective_id=1, has_side_effects=True, vmem_limit_bytes=LIMIT
        ),
        name="summed",
    )(kg)


def halves(x):
    high = x.astype(BF)
    return high, (x - high.astype(F32)).astype(BF)


def product(left, right):
    lh, ll = halves(left)
    rh, rl = halves(right)
    return jnp.dot(
        jnp.concatenate([lh, lh, ll], 1),
        jnp.concatenate([rh, rl, rh], 0),
        preferred_element_type=F32,
    )


def update_kernel(f0, f1, f2, kal, damping, out, g1, g2):
    g1[...] = jnp.zeros((256, 256), F32)
    g2[...] = jnp.zeros((256, 256), F32)
    full = (f0, f1, f2)
    for p in range(3):

        def gram(k, carry, p=p):
            high, low = halves(full[p][:, :, k].reshape(256, 256))
            turned = high.astype(F32).T.astype(BF)
            g1[...] += jnp.dot(turned, high, preferred_element_type=F32)
            g2[...] += jnp.dot(turned, low, preferred_element_type=F32)
            return carry

        lax.fori_loop(0, 9, gram, 0)
    cross = g2[...]
    total = g1[...] + (cross + cross.T)
    row = lax.broadcasted_iota(jnp.int32, (256, 256), 0)
    column = lax.broadcasted_iota(jnp.int32, (256, 256), 1)
    identity = jnp.where(row == column, 1.0, 0.0).astype(F32)

    def whole(x):
        return jnp.sum(jnp.sum(x, axis=1, keepdims=True), axis=0, keepdims=True)

    factor = total + (damping[0, 0] / 256.0) * whole(total * identity) * identity
    scale = 2.5 / jnp.sqrt(whole(factor * factor))
    root = jnp.sqrt(jnp.sqrt(scale)) * identity
    matrix = scale * factor

    def newton(step, carry):
        root, matrix = carry
        middle = (5.0 * identity - matrix) / 4.0
        root = product(root, middle)
        square = product(middle, middle)
        return root, product(square, product(square, matrix))

    root, matrix = lax.fori_loop(0, ITERS, newton, (root, matrix))
    energy = whole(root * product(total, root))
    size = jnp.sqrt(energy / (6912.0 * 256.0) + 1e-6)
    rate = 0.5 / size
    rh, rl = halves(root)
    stack = jnp.concatenate([rh, rl, rh], 0)
    for p in range(3):

        def write(k, carry, p=p):
            high, low = halves(full[p][:, :, k].reshape(256, 256))
            direction = jnp.dot(
                jnp.concatenate([high, high, low], 1), stack, preferred_element_type=F32
            )
            rows = pl.ds(pl.multiple_of((9 * p + k) * 256, 256), 256)
            out[rows, :] = (kal[rows, :].astype(F32) - rate * direction).astype(BF)
            return carry

        lax.fori_loop(0, 9, write, 0)


def update(f0, f1, f2, kal, damping):
    return pl.pallas_call(
        update_kernel,
        out_shape=jax.ShapeDtypeStruct((6912, 256), BF),
        in_specs=[pl.BlockSpec(memory_space=VMEM)] * 4 + [pl.BlockSpec(memory_space=pltpu.SMEM)],
        out_specs=pl.BlockSpec(memory_space=VMEM),
        scratch_shapes=[VMEM((256, 256), F32), VMEM((256, 256), F32)],
        compiler_params=pltpu.CompilerParams(vmem_limit_bytes=LIMIT),
        name="update",
    )(f0, f1, f2, kal, damping)


def on_device(activations, out_grad, kernel, damping):
    own = jnp.pad(kernel, ((0, 2), (0, 0))).reshape(7, 8, 256)
    gc, lc, rc, k0, k1, k2 = halo(out_grad, own)
    kg, ig, kal = conv(activations.reshape(2048, 256), gc, lc, rc, k0, k1, k2)
    f0, f1, f2 = summed(kg.reshape(27, 2, 4, 4, 8, 256))
    new_kernel = update(f0, f1, f2, kal, damping.reshape(1, 1))
    return ig.reshape(activations.shape), new_kernel


def solution(mesh):
    placed = (
        P("frame", "height", "width", None),
        P("frame", "height", "width", None),
        P(("frame", "height", "width"), None),
        P(),
    )
    return jax.shard_map(
        on_device,
        mesh=mesh,
        in_specs=placed,
        out_specs=(P("frame", "height", "width", None), P()),
        check_vma=False,
    )
```

```python
import functools

import jax
import jax.numpy as jnp
from jax import lax
from jax.experimental import pallas as pl
from jax.experimental.pallas import tpu as pltpu
from jax.sharding import PartitionSpec as P

MESH = pl.DeviceIdType.MESH
ITERS = 12
VMEM = pltpu.VMEM
BF = jnp.bfloat16
F32 = jnp.float32
LIMIT = 65000 * 1024
ORDERS = (("x", "y", "z"), ("y", "z", "x"), ("z", "x", "y"))
CUTS = ((0, 2), (2, 4), (4, 7))


def place():
    f, h, w = lax.axis_index("frame"), lax.axis_index("height"), lax.axis_index("width")
    return {"x": 2 * f + w % 2, "y": w // 2, "z": h // 2, "c": h % 2}


def device(at):
    return (at["x"] // 2, 2 * at["z"] + at["c"], 2 * at["y"] + at["x"] % 2)


def along(at, axis, k):
    moved = dict(at)
    moved[axis] = (at[axis] + k) % 4
    return device(moved)


def other_core(at):
    moved = dict(at)
    moved["c"] = 1 - at["c"]
    return device(moved)


def meet(partners):
    barrier = pltpu.get_barrier_semaphore()
    for partner in partners:
        pl.semaphore_signal(barrier, inc=1, device_id=partner, device_id_type=MESH)
    pl.semaphore_wait(barrier, len(partners))


def send(src, dst, sems, index, to):
    copy = pltpu.make_async_remote_copy(
        src_ref=src,
        dst_ref=dst,
        send_sem=sems[0].at[index],
        recv_sem=sems[1].at[index],
        device_id=to,
        device_id_type=MESH,
    )
    copy.start()
    return copy


def halves(x):
    high = x.astype(BF)
    return high, (x - high.astype(F32)).astype(BF)


def product(left, right):
    lh, ll = halves(left)
    rh, rl = halves(right)
    return jnp.dot(
        jnp.concatenate([lh, lh, ll], 1),
        jnp.concatenate([rh, rl, rh], 0),
        preferred_element_type=F32,
    )


def whole(x):
    return jnp.sum(jnp.sum(x, axis=1, keepdims=True), axis=0, keepdims=True)


N_SENDS = 9 + 30 + 51 + 11 + 27
SCRATCH = dict(
    gc=VMEM((5, 18, 32, 256), BF),
    lc=VMEM((5, 32, 256), BF),
    rc=VMEM((5, 32, 256), BF),
    edge=VMEM((2, 4, 32, 256), BF),
    k0=VMEM((2, 64, 2, 8, 256), BF),
    k1=VMEM((2, 64, 2, 8, 256), BF),
    k2=VMEM((2, 64, 3, 8, 256), BF),
    gs=VMEM((3, 6, 18, 32, 256), BF),
    lf=VMEM((5, 32, 256), F32),
    rf=VMEM((5, 32, 256), F32),
    act_t=VMEM((256, 2048), BF),
    mix=VMEM((432, 256), F32),
    kal=VMEM((6912, 256), BF),
    kg=VMEM((27, 2, 4, 4, 8, 256), F32),
    r0=VMEM((27, 1, 4, 4, 8, 256), F32),
    s1=VMEM((27, 4, 4, 8, 256), F32),
    ra=VMEM((3, 3, 9, 1, 4, 8, 256), F32),
    s2=VMEM((3, 9, 4, 8, 256), F32),
    rb=VMEM((3, 3, 9, 1, 8, 256), F32),
    s3=VMEM((3, 9, 8, 256), F32),
    r3=VMEM((3, 3, 9, 8, 256), F32),
    f0=VMEM((2, 16, 9, 8, 256), F32),
    f1=VMEM((2, 16, 9, 8, 256), F32),
    f2=VMEM((2, 16, 9, 8, 256), F32),
    gp=VMEM((3, 2, 64, 128), F32),
    gr0=VMEM((3, 64, 128), F32),
    ga=VMEM((3, 3, 64, 128), F32),
    gr=VMEM((3, 3, 3, 64, 128), F32),
    gfull=VMEM((2, 3, 64, 128), F32),
    total=VMEM((256, 256), F32),
    root=VMEM((256, 256), F32),
    matrix=VMEM((256, 256), F32),
    sems=pltpu.SemaphoreType.DMA((N_SENDS,)),
    rsems=pltpu.SemaphoreType.DMA((N_SENDS,)),
    lsem=pltpu.SemaphoreType.DMA((4,)),
)


class Refs:
    pass


def step_kernel(g, own, act, damping, ig, out, *scratch):
    r = Refs()
    for name, ref in zip(SCRATCH, scratch):
        setattr(r, name, ref)
    at = place()
    f, h, w = lax.axis_index("frame"), lax.axis_index("height"), lax.axis_index("width")
    up, down = (f, (h + 7) % 8, w), (f, (h + 1) % 8, w)
    left, right = (f, h, (w + 7) % 8), (f, h, (w + 1) % 8)
    across = (1 - f, h, w)
    core = at["c"]
    partner = other_core(at)
    parts, full = (r.k0, r.k1, r.k2), (r.f0, r.f1, r.f2)
    mine = [[at[axis] for axis in o] for o in ORDERS]
    sent = []

    def go(src, dst, to):
        copy = send(src, dst, (r.sems, r.rsems), len(sent), to)
        sent.append(copy)
        return copy

    def three(src, dst, p, s):
        return [go(src(k), dst(k), along(at, ORDERS[p][s], k)) for k in (1, 2, 3)]

    def landed(copies):
        for copy in copies:
            copy.wait_recv()

    index = [m[2] * 16 + m[1] * 4 + m[0] for m in mine]
    here = [pltpu.make_async_copy(g, r.gc.at[0:4, 1:17], r.lsem.at[0])]
    for p, (lo, hi) in enumerate(CUTS):
        here.append(
            pltpu.make_async_copy(own.at[lo:hi], parts[p].at[core, index[p]], r.lsem.at[1 + p])
        )
    for copy in here:
        copy.start()
    meet(
        [up, down, left, right, across, partner]
        + [along(at, axis, k) for axis in "xyz" for k in (1, 2, 3)]
    )
    last = 3 * (1 - f)
    rows = [
        go(g.at[:, 0:1], r.gc.at[0:4, 17:18], up),
        go(g.at[:, 15:16], r.gc.at[0:4, 0:1], down),
    ]
    face = [go(g.at[last], r.gc.at[4, 1:17], across)]
    gather = [
        three(lambda k: own.at[lo:hi], lambda k: parts[p].at[core, index[p]], p, 0)
        for p, (lo, hi) in enumerate(CUTS)
    ]
    for n in range(8):
        block = act[256 * n : 256 * n + 256, :].astype(F32)
        r.act_t[:, 256 * n : 256 * n + 256] = block.T.astype(BF)
    line = lax.broadcasted_iota(jnp.int32, (64, 576), 0)
    spot = lax.broadcasted_iota(jnp.int32, (64, 576), 1)
    want = jnp.where(line < 32, line * 32 + 31, (line - 32) * 32)
    pick = jnp.where(spot == want, 1.0, 0.0).astype(BF)
    here[0].wait()
    landed(rows)
    face += [
        go(r.gc.at[last, 0:1], r.gc.at[4, 0:1], across),
        go(r.gc.at[last, 17:18], r.gc.at[4, 17:18], across),
    ]
    for frame in range(4):
        block = r.gc[frame].reshape(576, 256)
        cut = jnp.dot(pick, block, preferred_element_type=F32).astype(BF)
        r.edge[0, frame] = cut[:32]
        r.edge[1, frame] = cut[32:]
    columns = [
        go(r.edge.at[0], r.lc.at[0:4], right),
        go(r.edge.at[1], r.rc.at[0:4], left),
    ]
    for copy in here[1:]:
        copy.wait()
    for p in range(3):
        landed(gather[p])
        held = parts[p].at[core, pl.ds(mine[p][2] * 16 + mine[p][1] * 4, 4)]
        gather[p] = three(lambda k: held, lambda k: held, p, 1)
    landed(columns)
    face += [
        go(r.lc.at[last], r.lc.at[4], across),
        go(r.rc.at[last], r.rc.at[4], across),
    ]

    sub = lax.broadcasted_iota(jnp.int32, (32, 256), 0)

    def build(n, carry):
        frame, row = n // 18, n % 18
        slot = jnp.where(frame == 4, 5 * (1 - f), frame + 1)
        off = jnp.logical_or(
            jnp.logical_and(row == 0, h == 0), jnp.logical_and(row == 17, h == 7)
        )
        keep = jnp.where(off, 0.0, 1.0)
        x = r.gc[frame, row].astype(F32) * keep
        before = r.lf[frame, pl.ds(row, 1), :] * keep
        after = r.rf[frame, pl.ds(row, 1), :] * keep
        r.gs[1, slot, row] = x.astype(BF)
        r.gs[0, slot, row] = jnp.where(sub == 31, after, pltpu.roll(x, 31, 0)).astype(BF)
        r.gs[2, slot, row] = jnp.where(sub == 0, before, pltpu.roll(x, 1, 0)).astype(BF)
        return carry

    def clear(n, carry):
        for c in range(3):
            r.gs[c, 5 * f, n] = jnp.zeros((32, 256), BF)
        return carry

    r.lf[0:4] = jnp.where(w == 0, 0.0, r.lc[0:4].astype(F32))
    r.rf[0:4] = jnp.where(w == 7, 0.0, r.rc[0:4].astype(F32))
    lax.fori_loop(0, 72, build, 0)
    lax.fori_loop(0, 18, clear, 0)
    for p in range(3):
        landed(gather[p])
        held = parts[p].at[core, pl.ds(mine[p][2] * 16, 16)]
        gather[p] = three(lambda k: held, lambda k: held, p, 2)

    def weight(t, carry):
        a, b, c = t // 9, (t // 3) % 3, t % 3
        s = r.gs[c, pl.ds(2 - a, 4), pl.ds(2 - b, 16)].reshape(2048, 256)
        r.kg[t] = jnp.dot(r.act_t[...], s, preferred_element_type=F32).reshape(2, 4, 4, 8, 256)
        return carry

    def swap(p):
        lax.fori_loop(9 * p, 9 * p + 9, weight, 0)
        rows = pl.ds(9 * p, 9)
        return go(r.kg.at[rows, pl.ds(1 - core, 1)], r.r0.at[rows], partner)

    def first(p, copy):
        copy.wait_recv()

        def add(t, carry):
            r.s1[t] = r.kg[t, core] + r.r0[t, 0]
            return carry

        lax.fori_loop(9 * p, 9 * p + 9, add, 0)
        rows = pl.ds(9 * p, 9)
        return three(
            lambda k: r.s1.at[rows, pl.ds((mine[p][0] + k) % 4, 1)],
            lambda k: r.ra.at[p, k - 1],
            p,
            0,
        )

    parted = [None] * 3
    swap1 = swap(1)
    landed(face)
    r.lf[4] = jnp.where(w == 0, 0.0, r.lc[4].astype(F32))
    r.rf[4] = jnp.where(w == 7, 0.0, r.rc[4].astype(F32))
    lax.fori_loop(72, 90, build, 0)
    swap0 = swap(0)
    parted[1] = first(1, swap1)
    swap2 = swap(2)
    parted[0] = first(0, swap0)
    for p in range(3):
        landed(gather[p])
        gather[p] = [go(parts[p].at[core], parts[p].at[core], partner)]
    parted[2] = first(2, swap2)

    def align(n, carry):
        x_hi, z, c = n // 8, (n // 2) % 4, n % 2
        for col in range(8):
            spot = {"x": 2 * x_hi + col % 2, "y": col // 2, "z": z}
            for p, (part, (lo, hi)) in enumerate(zip(parts, CUTS)):
                o = ORDERS[p]
                block = part[c, spot[o[2]] * 16 + spot[o[1]] * 4 + spot[o[0]]].astype(F32)
                for j in range(lo, hi):
                    size = 6 if j == 6 else 8
                    r.mix[54 * col + 8 * j : 54 * col + 8 * j + size] = block[j - lo][:size]
        r.kal[pl.ds(pl.multiple_of(n * 432, 432), 432), :] = r.mix[...].astype(BF)
        return carry

    def data(q, carry):
        taps = [
            r.gs[t % 3, q + 2 - t // 9, pl.ds(2 - (t // 3) % 3, 16)].reshape(512, 256)
            for t in range(27)
        ]
        sums = jnp.dot(jnp.concatenate(taps, 1), r.kal[...], preferred_element_type=F32)
        ig[pl.ds(pl.multiple_of(q * 512, 512), 512), :] = (
            sums / jnp.sqrt(jnp.float32(6912))
        ).astype(BF)
        return carry

    for p in range(3):
        landed(gather[p])
    lax.fori_loop(0, 16, align, 0)
    lax.fori_loop(0, 4, data, 0)

    for p in (1, 0, 2):
        landed(parted[p])

        def add(t, carry, p=p):
            r.s2[p, t] = (r.s1[9 * p + t, mine[p][0]] + r.ra[p, 1, t, 0]) + (
                r.ra[p, 0, t, 0] + r.ra[p, 2, t, 0]
            )
            return carry

        lax.fori_loop(0, 9, add, 0)
        parted[p] = three(
            lambda k: r.s2.at[p, :, pl.ds((mine[p][1] + k) % 4, 1)],
            lambda k: r.rb.at[p, k - 1],
            p,
            1,
        )
    for p in (1, 0, 2):
        landed(parted[p])

        def add(t, carry, p=p):
            r.s3[p, t] = (r.s2[p, t, mine[p][1]] + r.rb[p, 1, t, 0]) + (
                r.rb[p, 0, t, 0] + r.rb[p, 2, t, 0]
            )
            return carry

        lax.fori_loop(0, 9, add, 0)
        parted[p] = three(lambda k: r.s3.at[p], lambda k: r.r3.at[p, k - 1], p, 2)
    spots = [m[0] * 4 + m[1] for m in mine]
    for p in (1, 0, 2):
        landed(parted[p])

        def add(t, carry, p=p):
            full[p][core, spots[p], t] = (r.s3[p, t] + r.r3[p, 1, t]) + (
                r.r3[p, 0, t] + r.r3[p, 2, t]
            )
            return carry

        lax.fori_loop(0, 9, add, 0)

    x = jnp.concatenate([full[p][core, spots[p]].reshape(72, 256) for p in range(3)], 0)
    gram = 0.25 * lax.dot_general(
        x, x, (((0,), (0,)), ((), ())), precision=lax.Precision.HIGHEST, preferred_element_type=F32
    )
    for p, block in enumerate((gram[:128, :128], gram[:128, 128:], gram[128:, 128:])):
        r.gp[p] = block.reshape(2, 64, 128)
    halfgram = go(r.gp.at[:, 1 - core], r.gr0, partner)
    spread = []
    for p in range(3):
        held = full[p].at[core, pl.ds(spots[p], 1)]
        spread.append(three(lambda k: held, lambda k: held, p, 1))
    halfgram.wait_recv()
    r.ga[0] = r.gp[:, core] + r.gr0[...]
    for s in range(3):
        hops = [
            three(lambda k: r.ga.at[s, p], lambda k: r.gr.at[s, p, k - 1], p, s) for p in range(3)
        ]
        for p in range(3):
            landed(hops[p])
            value = (r.ga[s, p] + r.gr[s, p, 1]) + (r.gr[s, p, 0] + r.gr[s, p, 2])
            if s < 2:
                r.ga[s + 1, p] = value
            else:
                r.gfull[core, p] = value
    other = go(r.gfull.at[core], r.gfull.at[core], partner)
    for p in range(3):
        landed(spread[p])
        held = full[p].at[core, pl.ds(mine[p][0] * 4, 4)]
        spread[p] = three(lambda k: held, lambda k: held, p, 0)
    other.wait_recv()
    b0, b1, b2 = [r.gfull[:, p].reshape(128, 128) for p in range(3)]
    r.total[...] = jnp.concatenate(
        [jnp.concatenate([b0, b1], 1), jnp.concatenate([b1.T, b2], 1)], 0
    )

    row = lax.broadcasted_iota(jnp.int32, (256, 256), 0)
    column = lax.broadcasted_iota(jnp.int32, (256, 256), 1)
    identity = jnp.where(row == column, 1.0, 0.0).astype(F32)
    factor = r.total[...] + (damping[0, 0] / 256.0) * whole(r.total[...] * identity) * identity
    scale = 2.5 / jnp.sqrt(whole(factor * factor))
    r.root[...] = jnp.sqrt(jnp.sqrt(scale)) * identity
    r.matrix[...] = scale * factor

    def newton(n, carry):
        middle = (5.0 * identity - r.matrix[...]) / 4.0
        both = product(jnp.concatenate([r.root[...], middle], 0), middle)
        r.root[...] = both[:256]
        square = both[256:]
        r.matrix[...] = product(square, product(square, r.matrix[...]))
        return carry

    lax.fori_loop(0, ITERS - 3, newton, 0)
    for p in range(3):
        landed(spread[p])
        spread[p] = [go(full[p].at[core], full[p].at[core], partner)]
    lax.fori_loop(ITERS - 3, ITERS, newton, 0)
    root = r.root[...]
    energy = whole(root * product(r.total[...], root))
    size = jnp.sqrt(energy / (6912.0 * 256.0) + 1e-6)
    rate = 0.5 / size
    rh, rl = halves(root)
    stack = jnp.concatenate([rh, rl, rh], 0)
    for p in range(3):
        landed(spread[p])

        def write(k, carry, p=p):
            high, low = halves(full[p][:, :, k].reshape(256, 256))
            direction = jnp.dot(
                jnp.concatenate([high, high, low], 1), stack, preferred_element_type=F32
            )
            lines = pl.ds(pl.multiple_of((9 * p + k) * 256, 256), 256)
            out[lines, :] = (r.kal[lines, :].astype(F32) - rate * direction).astype(BF)
            return carry

        lax.fori_loop(0, 9, write, 0)
    for copy in sent:
        copy.wait_send()
    assert len(sent) <= N_SENDS, len(sent)


def step(g, own, act, damping):
    return pl.pallas_call(
        step_kernel,
        out_shape=(
            jax.ShapeDtypeStruct((2048, 256), BF),
            jax.ShapeDtypeStruct((6912, 256), BF),
        ),
        in_specs=[
            pl.BlockSpec(memory_space=pl.ANY),
            pl.BlockSpec(memory_space=pl.ANY),
            pl.BlockSpec(memory_space=VMEM),
            pl.BlockSpec(memory_space=pltpu.SMEM),
        ],
        out_specs=[pl.BlockSpec(memory_space=VMEM)] * 2,
        scratch_shapes=list(SCRATCH.values()),
        compiler_params=pltpu.CompilerParams(
            collective_id=0, has_side_effects=True, vmem_limit_bytes=LIMIT
        ),
        name="step",
    )(g, own, act, damping)


def on_device(activations, out_grad, kernel, damping):
    own = jnp.pad(kernel, ((0, 2), (0, 0))).reshape(7, 8, 256)
    ig, new_kernel = step(
        out_grad, own, activations.reshape(2048, 256), damping.reshape(1, 1)
    )
    return ig.reshape(activations.shape), new_kernel


def solution(mesh):
    placed = (
        P("frame", "height", "width", None),
        P("frame", "height", "width", None),
        P(("frame", "height", "width"), None),
        P(),
    )
    return jax.shard_map(
        on_device,
        mesh=mesh,
        in_specs=placed,
        out_specs=(P("frame", "height", "width", None), P()),
        check_vma=False,
    )
```

```python
import functools

import jax
import jax.numpy as jnp
from jax import lax
from jax.experimental import pallas as pl
from jax.experimental.pallas import tpu as pltpu
from jax.sharding import PartitionSpec as P

MESH = pl.DeviceIdType.MESH
ITERS = 12
ON, OVER = 4, 8
VMEM = pltpu.VMEM
BF = jnp.bfloat16
F32 = jnp.float32
LIMIT = 51 * 1024 * 1024
ORDERS = (("x", "y", "z"), ("y", "z", "x"), ("z", "x", "y"))
CUTS = ((0, 16), (16, 32), (32, 54))


def place():
    f, h, w = lax.axis_index("frame"), lax.axis_index("height"), lax.axis_index("width")
    return {"x": 2 * f + w % 2, "y": w // 2, "z": h // 2, "c": h % 2}


def device(at):
    return (at["x"] // 2, 2 * at["z"] + at["c"], 2 * at["y"] + at["x"] % 2)


def along(at, axis, k):
    moved = dict(at)
    moved[axis] = (at[axis] + k) % 4
    return device(moved)


def turn(at, b, s):
    which = (b + s) % 3
    return jnp.where(which == 0, at["x"], jnp.where(which == 1, at["y"], at["z"]))


def turned(at, b, s, k):
    which, moved = (b + s) % 3, dict(at)
    for n, axis in enumerate("xyz"):
        moved[axis] = jnp.where(which == n, (at[axis] + k) % 4, at[axis])
    return device(moved)


def other_core(at):
    moved = dict(at)
    moved["c"] = 1 - at["c"]
    return device(moved)


def meet(partners):
    barrier = pltpu.get_barrier_semaphore()
    for partner in partners:
        pl.semaphore_signal(barrier, inc=1, device_id=partner, device_id_type=MESH)
    pl.semaphore_wait(barrier, len(partners))


def halves(x):
    high = x.astype(BF)
    return high, (x - high.astype(F32)).astype(BF)


def product(left, right):
    lh, ll = halves(left)
    rh, rl = halves(right)
    return jnp.dot(
        jnp.concatenate([lh, lh, ll], 1),
        jnp.concatenate([rh, rl, rh], 0),
        preferred_element_type=F32,
    )


def whole(x):
    return jnp.sum(jnp.sum(x, axis=1, keepdims=True), axis=0, keepdims=True)


N_SENDS = 110
SCRATCH = dict(
    gc=VMEM((5, 18, 32, 256), BF),
    act=VMEM((2048, 256), BF),
    ownv=VMEM((54, 256), BF),
    o0=VMEM((16, 256), BF),
    o1=VMEM((16, 256), BF),
    o2=VMEM((24, 256), BF),
    lc=VMEM((5, 16, 256), BF),
    rc=VMEM((5, 16, 256), BF),
    edge=VMEM((2, 4, 16, 256), BF),
    spots=VMEM((4, 16, 256), F32),
    cs=VMEM((4, 16, 256), BF),
    cr=VMEM((4, 16, 256), BF),
    cf=VMEM((4, 16, 256), BF),
    k0=VMEM((2, 64, 16, 256), BF),
    k1=VMEM((2, 64, 16, 256), BF),
    k2=VMEM((2, 64, 24, 256), BF),
    gs=VMEM((3, 6, 18, 32, 256), BF),
    lf=VMEM((5, 18, 256), F32),
    rf=VMEM((5, 18, 256), F32),
    act_t=VMEM((256, 2048), BF),
    mix=VMEM((432, 256), F32),
    kal=VMEM((6912, 256), BF),
    kg=VMEM((9, 3, 2, 4, 4, 8, 256), F32),
    r0=VMEM((9, 3, 1, 4, 4, 8, 256), F32),
    s1=VMEM((9, 3, 4, 4, 8, 256), F32),
    ra=VMEM((9, 3, 3, 1, 4, 8, 256), F32),
    s2=VMEM((9, 3, 4, 8, 256), F32),
    rb=VMEM((9, 3, 3, 1, 8, 256), F32),
    s3=VMEM((9, 3, 8, 256), F32),
    r3=VMEM((9, 3, 3, 8, 256), F32),
    full=VMEM((3, 2, 16, 3, 3, 8, 256), F32),
    pages=VMEM((2, 768, 256), BF),
    psem=pltpu.SemaphoreType.DMA((2,)),
    z=pltpu.SemaphoreType.DMA((2, 9)),
    y1=pltpu.SemaphoreType.DMA((2, 27)),
    y2=pltpu.SemaphoreType.DMA((2, 27)),
    y3=pltpu.SemaphoreType.DMA((2, 27)),
    gp=VMEM((3, 2, 64, 128), F32),
    gr0=VMEM((3, 64, 128), F32),
    ga=VMEM((4, 3, 64, 128), F32),
    y4=pltpu.SemaphoreType.DMA((2, 27)),
    gr=VMEM((3, 3, 3, 64, 128), F32),
    gfull=VMEM((2, 3, 64, 128), F32),
    total=VMEM((256, 256), F32),
    root=VMEM((256, 256), F32),
    matrix=VMEM((256, 256), F32),
    igv=VMEM((2048, 256), BF),
    sems=pltpu.SemaphoreType.DMA((N_SENDS,)),
    rsems=pltpu.SemaphoreType.DMA((N_SENDS,)),
    lsem=pltpu.SemaphoreType.DMA((16,)),
)


class Refs:
    pass


def step_kernel(g, own, act, damping, ig, out, *scratch):
    r = Refs()
    for name, ref in zip(SCRATCH, scratch):
        setattr(r, name, ref)
    at = place()
    f, h, w = lax.axis_index("frame"), lax.axis_index("height"), lax.axis_index("width")
    hu, hd, wl, wr = (h + 7) % 8, (h + 1) % 8, (w + 7) % 8, (w + 1) % 8
    up, down, left, right = (f, hu, w), (f, hd, w), (f, h, wl), (f, h, wr)
    across = (1 - f, h, w)
    corners = [(f, hd, wr), (f, hd, wl), (f, hu, wr), (f, hu, wl)]
    core = at["c"]
    partner = other_core(at)
    parts = (r.k0, r.k1, r.k2)
    mine = [[at[axis] for axis in o] for o in ORDERS]
    sent, kept = [], []

    def plan(src, dst, to):
        n = len(sent)
        sent.append(
            pltpu.make_async_remote_copy(
                src_ref=src,
                dst_ref=dst,
                send_sem=r.sems.at[n],
                recv_sem=r.rsems.at[n],
                device_id=to,
                device_id_type=MESH,
            )
        )
        return sent[-1]

    def go(src, dst, to):
        copy = plan(src, dst, to)
        copy.start()
        return copy

    def keep(src, dst):
        copy = pltpu.make_async_copy(src, dst, r.lsem.at[len(kept)])
        copy.start()
        kept.append(copy)
        return copy

    def three(src, dst, p, s):
        return [go(src(k), dst(k), along(at, ORDERS[p][s], k)) for k in (1, 2, 3)]

    def landed(copies):
        for copy in copies:
            copy.wait_recv()

    index = [m[2] * 16 + m[1] * 4 + m[0] for m in mine]
    inside = keep(g, r.gc.at[0:4, 1:17])
    flat = keep(act, r.act)
    held_rows = keep(own, r.ownv)
    meet(
        [up, down, left, right, across, partner]
        + corners
        + [along(at, axis, k) for axis in "xyz" for k in (1, 2, 3)]
    )
    last = 3 * (1 - f)
    near = [
        go(g.at[:, 0:1], r.gc.at[0:4, 17:18], up),
        go(g.at[:, 15:16], r.gc.at[0:4, 0:1], down),
    ]
    face = [go(g.at[last], r.gc.at[4, 1:17], across)]
    line = lax.broadcasted_iota(jnp.int32, (32, 512), 0)
    spot = lax.broadcasted_iota(jnp.int32, (32, 512), 1)
    want = jnp.where(line < 16, line * 32 + 31, (line - 16) * 32)
    pick = jnp.where(spot == want, 1.0, 0.0).astype(BF)
    r.spots[...] = jnp.zeros((4, 16, 256), F32)
    held_rows.wait()
    r.o0[...] = r.ownv[0:16, :]
    r.o1[...] = r.ownv[16:32, :]
    r.mix[0:24, :] = jnp.zeros((24, 256), F32)
    r.mix[0:22, :] = r.ownv[32:54, :].astype(F32)
    r.o2[...] = r.mix[0:24, :].astype(BF)
    gather = []
    for p, rows in enumerate((r.o0, r.o1, r.o2)):
        keep(rows, parts[p].at[core, index[p]])
        gather.append(three(lambda k: rows, lambda k: parts[p].at[core, index[p]], p, 0))
    inside.wait()
    for frame in range(4):
        block = r.gc[frame, 1:17].reshape(512, 256)
        cut = jnp.dot(pick, block, preferred_element_type=F32)
        r.edge[0, frame] = cut[:16].astype(BF)
        r.edge[1, frame] = cut[16:].astype(BF)
        for kind, n in enumerate((15, 31, 0, 16)):
            r.spots[kind, frame : frame + 1, :] = cut[n : n + 1]
    r.cs[...] = r.spots[...].astype(BF)
    near += [
        go(r.edge.at[0], r.lc.at[0:4], right),
        go(r.edge.at[1], r.rc.at[0:4], left),
    ] + [go(r.cs.at[kind], r.cr.at[kind], to) for kind, to in enumerate(corners)]
    flat.wait()

    def flip(n, carry):
        rows = pl.ds(pl.multiple_of(256 * n, 256), 256)
        r.act_t[:, rows] = r.act[rows, :].astype(F32).T.astype(BF)
        return carry

    lax.fori_loop(0, 8, flip, 0)
    for copy in kept[3:6]:
        copy.wait()
    for p in range(3):
        landed(gather[p])
        held = parts[p].at[core, pl.ds(mine[p][2] * 16 + mine[p][1] * 4, 4)]
        gather[p] = three(lambda k: held, lambda k: held, p, 1)
    landed(near)
    face += [
        go(r.gc.at[last, 0:1], r.gc.at[4, 0:1], across),
        go(r.gc.at[last, 17:18], r.gc.at[4, 17:18], across),
        go(r.lc.at[last], r.lc.at[4], across),
        go(r.rc.at[last], r.rc.at[4], across),
        go(r.cr, r.cf, across),
    ]

    sub = lax.broadcasted_iota(jnp.int32, (32, 256), 0)

    def build(n, carry):
        frame, row = n // 18, n % 18
        slot = jnp.where(frame == 4, 5 * (1 - f), frame + 1)
        off = jnp.logical_or(
            jnp.logical_and(row == 0, h == 0), jnp.logical_and(row == 17, h == 7)
        )
        keep = jnp.where(off, 0.0, 1.0)
        x = r.gc[frame, row].astype(F32) * keep
        before = r.lf[frame, pl.ds(row, 1), :] * keep
        after = r.rf[frame, pl.ds(row, 1), :] * keep
        r.gs[1, slot, row] = x.astype(BF)
        r.gs[0, slot, row] = jnp.where(sub == 31, after, pltpu.roll(x, 31, 0)).astype(BF)
        r.gs[2, slot, row] = jnp.where(sub == 0, before, pltpu.roll(x, 1, 0)).astype(BF)
        return carry

    def clear(n, carry):
        for c in range(3):
            r.gs[c, 5 * f, n] = jnp.zeros((32, 256), BF)
        return carry

    def border(frame, corner):
        for side, columns, wide, edge in ((0, r.lc, r.lf, 0), (1, r.rc, r.rf, 7)):
            out = w == edge
            wide[frame, 1:17, :] = jnp.where(out, 0.0, columns[frame].astype(F32))
            wide[frame, 0:1, :] = jnp.where(out, 0.0, corner(side))
            wide[frame, 17:18, :] = jnp.where(out, 0.0, corner(2 + side))

    for frame in range(4):
        border(frame, lambda kind: r.cr[kind].astype(F32)[frame : frame + 1])
    lax.fori_loop(0, 72, build, 0)
    lax.fori_loop(0, 18, clear, 0)

    def turn_of(n):
        return jnp.where(n < 3, 3 + n, jnp.where((n < 6) == (f == 0), 6 + n % 3, n % 3))

    def nth(n):
        return jnp.where(n < 3, n + 3, jnp.where(n < 6, n - 3, n))

    def remote(src, dst, sems, n, to):
        return pltpu.make_async_remote_copy(
            src_ref=src,
            dst_ref=dst,
            send_sem=sems.at[0, n],
            recv_sem=sems.at[1, n],
            device_id=to,
            device_id_type=MESH,
        )

    def swaps(n):
        return [remote(r.kg.at[n, :, pl.ds(1 - core, 1)], r.r0.at[n], r.z, n, partner)]

    def firsts(n):
        b = n % 3
        return [
            remote(
                r.s1.at[n, :, pl.ds((turn(at, b, 0) + k) % 4, 1)],
                r.ra.at[n, k - 1],
                r.y1,
                3 * n + k - 1,
                turned(at, b, 0, k),
            )
            for k in (1, 2, 3)
        ]

    def seconds(n):
        b = n % 3
        return [
            remote(
                r.s2.at[n, :, pl.ds((turn(at, b, 1) + k) % 4, 1)],
                r.rb.at[n, k - 1],
                r.y2,
                3 * n + k - 1,
                turned(at, b, 1, k),
            )
            for k in (1, 2, 3)
        ]

    def thirds(n):
        return [
            remote(r.s3.at[n], r.r3.at[n, k - 1], r.y3, 3 * n + k - 1, turned(at, n % 3, 2, k))
            for k in (1, 2, 3)
        ]

    def start(copies):
        for copy in copies:
            copy.start()

    def weight(n):
        a, b = n // 3, n % 3
        s = jnp.concatenate(
            [r.gs[c, pl.ds(2 - a, 4), pl.ds(2 - b, 16)].reshape(2048, 256) for c in range(3)], 1
        )
        taps = jnp.dot(r.act_t[...], s, preferred_element_type=F32)
        for c in range(3):
            r.kg[n, c] = taps[:, 256 * c : 256 * c + 256].reshape(2, 4, 4, 8, 256)
        start(swaps(n))

    def first(n):
        landed(swaps(n))
        for c in range(3):
            r.s1[n, c] = r.kg[n, c, core] + r.r0[n, c, 0]
        start(firsts(n))

    def second(i, carry):
        n = nth(i)
        landed(firsts(n))
        mine_a = turn(at, n % 3, 0)
        for c in range(3):
            r.s2[n, c] = (r.s1[n, c, mine_a] + r.ra[n, 1, c, 0]) + (
                r.ra[n, 0, c, 0] + r.ra[n, 2, c, 0]
            )
        start(seconds(n))
        return carry

    def third(i, carry):
        n = nth(i)
        landed(seconds(n))
        mine_b = turn(at, n % 3, 1)
        for c in range(3):
            r.s3[n, c] = (r.s2[n, c, mine_b] + r.rb[n, 1, c, 0]) + (
                r.rb[n, 0, c, 0] + r.rb[n, 2, c, 0]
            )
        start(thirds(n))
        return carry

    def fourth(i, carry):
        n = nth(i)
        landed(thirds(n))
        a, b = n // 3, n % 3
        r.full[b, core, turn(at, b, 0) * 4 + turn(at, b, 1), a] = (r.s3[n] + r.r3[n, 1]) + (
            r.r3[n, 0] + r.r3[n, 2]
        )
        return carry

    widest = []
    for p in range(3):
        held = parts[p].at[core, pl.ds(mine[p][2] * 16, 16)]
        widest.append([plan(held, held, along(at, ORDERS[p][2], k)) for k in (1, 2, 3)])

    for p in range(3):
        landed(gather[p])
        start(widest[p])

    def chunk(n, carry):
        @pl.when(n == 6)
        def _():
            landed(face)
            far = [
                jnp.where(f == 0, r.cf[kind].astype(F32)[0:1], r.cf[kind].astype(F32)[3:4])
                for kind in range(4)
            ]
            border(4, lambda kind: far[kind])
            lax.fori_loop(72, 90, build, 0)

        @pl.when(n < 9)
        def _():
            weight(turn_of(n))

        @pl.when(n >= 1)
        def _():
            first(turn_of(n - 1))

        return carry

    lax.fori_loop(0, 10, chunk, 0)
    lax.fori_loop(0, 6, second, 0)
    lax.fori_loop(0, 3, third, 0)
    lax.fori_loop(6, 9, second, 0)
    lax.fori_loop(3, 6, third, 0)
    for p in range(3):
        landed(widest[p])
        gather[p] = [go(parts[p].at[core], parts[p].at[core], partner)]
    lax.fori_loop(0, 3, fourth, 0)
    lax.fori_loop(6, 9, third, 0)
    lax.fori_loop(3, 9, fourth, 0)

    def align(n, carry):
        x_hi, z, c = n // 8, (n // 2) % 4, n % 2
        for col in range(8):
            spot = {"x": 2 * x_hi + col % 2, "y": col // 2, "z": z}
            for p, (part, (lo, hi)) in enumerate(zip(parts, CUTS)):
                o = ORDERS[p]
                block = part[c, spot[o[2]] * 16 + spot[o[1]] * 4 + spot[o[0]]].astype(F32)
                r.mix[54 * col + lo : 54 * col + hi] = block[: hi - lo]
        r.kal[pl.ds(pl.multiple_of(n * 432, 432), 432), :] = r.mix[...].astype(BF)
        return carry

    def data(q, carry):
        taps = [
            r.gs[t % 3, q + 2 - t // 9, pl.ds(2 - (t // 3) % 3, 16)].reshape(512, 256)
            for t in range(27)
        ]
        sums = jnp.dot(jnp.concatenate(taps, 1), r.kal[...], preferred_element_type=F32)
        r.igv[pl.ds(pl.multiple_of(q * 512, 512), 512), :] = (
            sums / jnp.sqrt(jnp.float32(6912))
        ).astype(BF)
        return carry

    x = jnp.concatenate(
        [r.full[p, core, mine[p][0] * 4 + mine[p][1]].reshape(72, 256) for p in range(3)], 0
    )
    high, low = halves(x)
    grams = jnp.dot(
        x.T.astype(BF), jnp.concatenate([high, low], 1), preferred_element_type=F32
    )
    gram = 0.25 * (grams[:, :256] + (grams[:, 256:] + grams[:, 256:].T))
    for p, block in enumerate((gram[:128, :128], gram[:128, 128:], gram[128:, 128:])):
        r.gp[p] = block.reshape(2, 64, 128)
    halfgram = go(r.gp.at[:, 1 - core], r.gr0, partner)
    spread = []
    for p in range(3):
        held = r.full.at[p, core, mine[p][0] * 4 + mine[p][1]]
        spread.append(three(lambda k: held, lambda k: held, p, 1))
    for p in range(3):
        landed(gather[p])
    lax.fori_loop(0, 16, align, 0)
    landed([halfgram])
    r.ga[0] = r.gp[:, core] + r.gr0[...]

    def sums(n, carry):
        hops = [
            [
                remote(r.ga.at[n, p], r.gr.at[n, p, k - 1], r.y4, 9 * n + 3 * p + k - 1, turned(at, p, n, k))
                for k in (1, 2, 3)
            ]
            for p in range(3)
        ]
        for p in range(3):
            start(hops[p])
        data(n, 0)
        for p in range(3):
            landed(hops[p])
            r.ga[n + 1, p] = (r.ga[n, p] + r.gr[n, p, 1]) + (r.gr[n, p, 0] + r.gr[n, p, 2])
        for p in range(3):
            for copy in hops[p]:
                copy.wait_send()
        return carry

    lax.fori_loop(0, 3, sums, 0)
    r.gfull[core] = r.ga[3]
    other = go(r.gfull.at[core], r.gfull.at[core], partner)
    for p in range(3):
        landed(spread[p])
        held = r.full.at[p, core, pl.ds(mine[p][0] * 4, 4)]
        spread[p] = [
            go(held, held, along(at, ORDERS[p][0], 1)),
            go(held, held, along(at, ORDERS[p][0], 3)),
        ]
    data(3, 0)
    keep_ig = keep(r.igv, ig)
    landed([other])
    b0, b1, b2 = [r.gfull[:, p].reshape(128, 128) for p in range(3)]
    r.total[...] = jnp.concatenate(
        [jnp.concatenate([b0, b1], 1), jnp.concatenate([b1.T, b2], 1)], 0
    )

    row = lax.broadcasted_iota(jnp.int32, (256, 256), 0)
    column = lax.broadcasted_iota(jnp.int32, (256, 256), 1)
    identity = jnp.where(row == column, 1.0, 0.0).astype(F32)
    factor = r.total[...] + (damping[0, 0] / 256.0) * whole(r.total[...] * identity) * identity
    scale = 2.5 / jnp.sqrt(whole(factor * factor))
    r.root[...] = jnp.sqrt(jnp.sqrt(scale)) * identity
    r.matrix[...] = scale * factor

    relayed, doubled = [], []
    for p in range(3):
        before = r.full.at[p, core, pl.ds((mine[p][0] + 3) % 4 * 4, 2)]
        after = r.full.at[p, core, pl.ds((mine[p][0] + 1) % 4 * 4 + 2, 2)]
        relayed.append(
            [
                plan(before, before, along(at, ORDERS[p][0], 1)),
                plan(after, after, along(at, ORDERS[p][0], 3)),
            ]
        )
        doubled.append(plan(r.full.at[p, core], r.full.at[p, core], partner))

    def newton(n, carry):
        middle = (5.0 * identity - r.matrix[...]) / 4.0
        r.root[...] = product(r.root[...], middle)
        square = product(middle, middle)
        r.matrix[...] = product(square, product(square, r.matrix[...]))

        @pl.when(n == ON)
        def _():
            for p in range(3):
                landed(spread[p])
                start(relayed[p])

        @pl.when(n == OVER)
        def _():
            for p in range(3):
                landed(relayed[p])
                doubled[p].start()

        return carry

    lax.fori_loop(0, ITERS, newton, 0)
    root = r.root[...]
    energy = whole(root * product(r.total[...], root))
    size = jnp.sqrt(energy / (6912.0 * 256.0) + 1e-6)
    rh, rl = halves(root * (0.5 / size))
    stack = jnp.concatenate([rh, rl, rh], 0)

    def page(n):
        return pltpu.make_async_copy(
            r.pages.at[n % 2],
            out.at[pl.ds(pl.multiple_of(n * 768, 768), 768)],
            r.psem.at[n % 2],
        )

    def write(n, carry):
        @pl.when(n >= 2)
        def _():
            page(n - 2).wait()

        high, low = halves(
            jnp.concatenate(
                [r.full[n % 3, :, :, n // 3, c].reshape(256, 256) for c in range(3)], 0
            )
        )
        direction = jnp.dot(
            jnp.concatenate([high, high, low], 1), stack, preferred_element_type=F32
        )
        old = r.kal[pl.ds(pl.multiple_of(n * 768, 768), 768), :].astype(F32)
        r.pages[n % 2] = (old - direction).astype(BF)
        page(n).start()
        return carry

    landed(doubled)
    lax.fori_loop(0, 9, write, 0)
    page(7).wait()
    page(8).wait()
    keep_ig.wait()
    for copy in sent:
        copy.wait_send()

    def drain(n, carry):
        for copy in swaps(n) + firsts(n) + seconds(n) + thirds(n):
            copy.wait_send()
        return carry

    lax.fori_loop(0, 9, drain, 0)
    assert len(sent) <= N_SENDS, len(sent)


def step(g, own, act, damping):
    return pl.pallas_call(
        step_kernel,
        out_shape=(VMEM((2048, 256), BF), VMEM((6912, 256), BF)),
        in_specs=[pl.BlockSpec(memory_space=pl.ANY)] * 3
        + [pl.BlockSpec(memory_space=pltpu.SMEM)],
        out_specs=[pl.BlockSpec(memory_space=pl.ANY)] * 2,
        scratch_shapes=list(SCRATCH.values()),
        compiler_params=pltpu.CompilerParams(
            collective_id=0, has_side_effects=True, vmem_limit_bytes=LIMIT
        ),
        name="step",
    )(g, own, act, damping)


def on_device(activations, out_grad, kernel, damping):
    ig, new = step(
        out_grad, kernel, activations.reshape(2048, 256), damping.reshape(1, 1)
    )
    return ig.reshape(activations.shape), new


def solution(mesh):
    placed = (
        P("frame", "height", "width", None),
        P("frame", "height", "width", None),
        P(("frame", "height", "width"), None),
        P(),
    )
    return jax.shard_map(
        on_device,
        mesh=mesh,
        in_specs=placed,
        out_specs=(P("frame", "height", "width", None), P()),
        check_vma=False,
    )
```

```python
import functools

import jax
import jax.numpy as jnp
from jax import lax
from jax.experimental import pallas as pl
from jax.experimental.pallas import tpu as pltpu
from jax.sharding import PartitionSpec as P

MESH = pl.DeviceIdType.MESH
ITERS = 12
AG, ON = 2, 5
VMEM = pltpu.VMEM
BF = jnp.bfloat16
F32 = jnp.float32
LIMIT = 51 * 1024 * 1024
ORDERS = (("x", "y", "z"), ("y", "z", "x"), ("z", "x", "y"))
CUTS = ((0, 16), (16, 32), (32, 54))


def place():
    f, h, w = lax.axis_index("frame"), lax.axis_index("height"), lax.axis_index("width")
    return {"x": 2 * f + w % 2, "y": w // 2, "z": h // 2, "c": h % 2}


def device(at):
    return (at["x"] // 2, 2 * at["z"] + at["c"], 2 * at["y"] + at["x"] % 2)


def along(at, axis, k):
    moved = dict(at)
    moved[axis] = (at[axis] + k) % 4
    return device(moved)


def turn(at, b, s):
    which = (b + s) % 3
    if isinstance(which, int):
        return at["xyz"[which]]
    return jnp.where(which == 0, at["x"], jnp.where(which == 1, at["y"], at["z"]))


def turned(at, b, s, k):
    which, moved = (b + s) % 3, dict(at)
    if isinstance(which, int):
        return along(at, "xyz"[which], k)
    for n, axis in enumerate("xyz"):
        moved[axis] = jnp.where(which == n, (at[axis] + k) % 4, at[axis])
    return device(moved)


def other_core(at):
    moved = dict(at)
    moved["c"] = 1 - at["c"]
    return device(moved)


def meet(partners):
    barrier = pltpu.get_barrier_semaphore()
    for partner in partners:
        pl.semaphore_signal(barrier, inc=1, device_id=partner, device_id_type=MESH)
    pl.semaphore_wait(barrier, len(partners))


def halves(x):
    high = x.astype(BF)
    return high, (x - high.astype(F32)).astype(BF)


def product(left, right):
    lh, ll = halves(left)
    rh, rl = halves(right)
    return jnp.dot(
        jnp.concatenate([lh, lh, ll], 1),
        jnp.concatenate([rh, rl, rh], 0),
        preferred_element_type=F32,
    )


def whole(x):
    return jnp.sum(jnp.sum(x, axis=1, keepdims=True), axis=0, keepdims=True)


N_SENDS = 110
SCRATCH = dict(
    gc=VMEM((5, 18, 32, 256), BF),
    act=VMEM((2048, 256), BF),
    ownv=VMEM((54, 256), BF),
    o0=VMEM((16, 256), BF),
    o1=VMEM((16, 256), BF),
    o2=VMEM((24, 256), BF),
    lc=VMEM((5, 16, 256), BF),
    rc=VMEM((5, 16, 256), BF),
    edge=VMEM((2, 4, 16, 256), BF),
    spots=VMEM((4, 16, 256), F32),
    cs=VMEM((4, 16, 256), BF),
    cr=VMEM((4, 16, 256), BF),
    cf=VMEM((4, 16, 256), BF),
    k0=VMEM((2, 64, 16, 256), BF),
    k1=VMEM((2, 64, 16, 256), BF),
    k2=VMEM((2, 64, 24, 256), BF),
    gs=VMEM((3, 6, 18, 32, 256), BF),
    lf=VMEM((5, 18, 256), F32),
    rf=VMEM((5, 18, 256), F32),
    act_t=VMEM((256, 2048), BF),
    mix=VMEM((432, 256), F32),
    kal=VMEM((6912, 256), BF),
    kg=VMEM((9, 3, 2, 4, 4, 8, 256), F32),
    r0=VMEM((9, 3, 1, 4, 4, 8, 256), F32),
    s1=VMEM((9, 3, 4, 4, 8, 256), F32),
    ra=VMEM((9, 3, 3, 1, 4, 8, 256), F32),
    s2=VMEM((9, 3, 4, 8, 256), F32),
    rb=VMEM((9, 3, 3, 1, 8, 256), F32),
    s3=VMEM((9, 3, 8, 256), F32),
    r3=VMEM((9, 3, 3, 8, 256), F32),
    full=VMEM((3, 2, 16, 3, 3, 8, 256), F32),
    pages=VMEM((9, 3, 128, 256), BF),
    psem=pltpu.SemaphoreType.DMA((9,)),
    y5=pltpu.SemaphoreType.DMA((2, 9)),
    z=pltpu.SemaphoreType.DMA((2, 9)),
    y1=pltpu.SemaphoreType.DMA((2, 27)),
    y2=pltpu.SemaphoreType.DMA((2, 27)),
    y3=pltpu.SemaphoreType.DMA((2, 27)),
    gp=VMEM((3, 2, 64, 128), F32),
    gr0=VMEM((3, 64, 128), F32),
    ga=VMEM((4, 3, 64, 128), F32),
    y4=pltpu.SemaphoreType.DMA((2, 27)),
    gr=VMEM((3, 3, 3, 64, 128), F32),
    gfull=VMEM((2, 3, 64, 128), F32),
    total=VMEM((256, 256), F32),
    root=VMEM((256, 256), F32),
    matrix=VMEM((256, 256), F32),
    igv=VMEM((2048, 256), BF),
    sems=pltpu.SemaphoreType.DMA((N_SENDS,)),
    rsems=pltpu.SemaphoreType.DMA((N_SENDS,)),
    lsem=pltpu.SemaphoreType.DMA((16,)),
)


class Refs:
    pass


def step_kernel(g, own, act, damping, ig, out, *scratch):
    r = Refs()
    for name, ref in zip(SCRATCH, scratch):
        setattr(r, name, ref)
    at = place()
    f, h, w = lax.axis_index("frame"), lax.axis_index("height"), lax.axis_index("width")
    hu, hd, wl, wr = (h + 7) % 8, (h + 1) % 8, (w + 7) % 8, (w + 1) % 8
    up, down, left, right = (f, hu, w), (f, hd, w), (f, h, wl), (f, h, wr)
    across = (1 - f, h, w)
    corners = [(f, hd, wr), (f, hd, wl), (f, hu, wr), (f, hu, wl)]
    core = at["c"]
    partner = other_core(at)
    parts = (r.k0, r.k1, r.k2)
    mine = [[at[axis] for axis in o] for o in ORDERS]
    sent, kept = [], []

    def plan(src, dst, to):
        n = len(sent)
        sent.append(
            pltpu.make_async_remote_copy(
                src_ref=src,
                dst_ref=dst,
                send_sem=r.sems.at[n],
                recv_sem=r.rsems.at[n],
                device_id=to,
                device_id_type=MESH,
            )
        )
        return sent[-1]

    def go(src, dst, to):
        copy = plan(src, dst, to)
        copy.start()
        return copy

    def keep(src, dst):
        copy = pltpu.make_async_copy(src, dst, r.lsem.at[len(kept)])
        copy.start()
        kept.append(copy)
        return copy

    def three(src, dst, p, s):
        return [go(src(k), dst(k), along(at, ORDERS[p][s], k)) for k in (1, 2, 3)]

    def landed(copies):
        for copy in copies:
            copy.wait_recv()

    index = [m[2] * 16 + m[1] * 4 + m[0] for m in mine]
    inside = keep(g, r.gc.at[0:4, 1:17])
    flat = keep(act, r.act)
    held_rows = keep(own, r.ownv)
    meet(
        [up, down, left, right, across, partner]
        + corners
        + [along(at, axis, k) for axis in "xyz" for k in (1, 2, 3)]
    )
    last = 3 * (1 - f)
    near = [
        go(g.at[:, 0:1], r.gc.at[0:4, 17:18], up),
        go(g.at[:, 15:16], r.gc.at[0:4, 0:1], down),
    ]
    face = [go(g.at[last], r.gc.at[4, 1:17], across)]
    line = lax.broadcasted_iota(jnp.int32, (32, 512), 0)
    spot = lax.broadcasted_iota(jnp.int32, (32, 512), 1)
    want = jnp.where(line < 16, line * 32 + 31, (line - 16) * 32)
    pick = jnp.where(spot == want, 1.0, 0.0).astype(BF)
    r.spots[...] = jnp.zeros((4, 16, 256), F32)
    held_rows.wait()
    r.o0[...] = r.ownv[0:16, :]
    r.o1[...] = r.ownv[16:32, :]
    r.mix[0:24, :] = jnp.zeros((24, 256), F32)
    r.mix[0:22, :] = r.ownv[32:54, :].astype(F32)
    r.o2[...] = r.mix[0:24, :].astype(BF)
    gather = []
    for p, rows in enumerate((r.o0, r.o1, r.o2)):
        keep(rows, parts[p].at[core, index[p]])
        gather.append(three(lambda k: rows, lambda k: parts[p].at[core, index[p]], p, 0))
    inside.wait()
    for frame in range(4):
        block = r.gc[frame, 1:17].reshape(512, 256)
        cut = jnp.dot(pick, block, preferred_element_type=F32)
        r.edge[0, frame] = cut[:16].astype(BF)
        r.edge[1, frame] = cut[16:].astype(BF)
        for kind, n in enumerate((15, 31, 0, 16)):
            r.spots[kind, frame : frame + 1, :] = cut[n : n + 1]
    r.cs[...] = r.spots[...].astype(BF)
    near += [
        go(r.edge.at[0], r.lc.at[0:4], right),
        go(r.edge.at[1], r.rc.at[0:4], left),
    ] + [go(r.cs.at[kind], r.cr.at[kind], to) for kind, to in enumerate(corners)]
    flat.wait()

    def flip(n, carry):
        rows = pl.ds(pl.multiple_of(256 * n, 256), 256)
        r.act_t[:, rows] = r.act[rows, :].astype(F32).T.astype(BF)
        return carry

    lax.fori_loop(0, 8, flip, 0)
    for copy in kept[3:6]:
        copy.wait()
    for p in range(3):
        landed(gather[p])
        held = parts[p].at[core, pl.ds(mine[p][2] * 16 + mine[p][1] * 4, 4)]
        gather[p] = three(lambda k: held, lambda k: held, p, 1)
    landed(near)
    face += [
        go(r.gc.at[last, 0:1], r.gc.at[4, 0:1], across),
        go(r.gc.at[last, 17:18], r.gc.at[4, 17:18], across),
        go(r.lc.at[last], r.lc.at[4], across),
        go(r.rc.at[last], r.rc.at[4], across),
        go(r.cr, r.cf, across),
    ]

    sub = lax.broadcasted_iota(jnp.int32, (32, 256), 0)

    def build(n, carry):
        frame, row = n // 18, n % 18
        slot = jnp.where(frame == 4, 5 * (1 - f), frame + 1)
        off = jnp.logical_or(
            jnp.logical_and(row == 0, h == 0), jnp.logical_and(row == 17, h == 7)
        )
        keep = jnp.where(off, 0.0, 1.0)
        x = r.gc[frame, row].astype(F32) * keep
        before = r.lf[frame, pl.ds(row, 1), :] * keep
        after = r.rf[frame, pl.ds(row, 1), :] * keep
        r.gs[1, slot, row] = x.astype(BF)
        r.gs[0, slot, row] = jnp.where(sub == 31, after, pltpu.roll(x, 31, 0)).astype(BF)
        r.gs[2, slot, row] = jnp.where(sub == 0, before, pltpu.roll(x, 1, 0)).astype(BF)
        return carry

    def clear(n, carry):
        for c in range(3):
            r.gs[c, 5 * f, n] = jnp.zeros((32, 256), BF)
        return carry

    def border(frame, corner):
        for side, columns, wide, edge in ((0, r.lc, r.lf, 0), (1, r.rc, r.rf, 7)):
            out = w == edge
            wide[frame, 1:17, :] = jnp.where(out, 0.0, columns[frame].astype(F32))
            wide[frame, 0:1, :] = jnp.where(out, 0.0, corner(side))
            wide[frame, 17:18, :] = jnp.where(out, 0.0, corner(2 + side))

    for frame in range(4):
        border(frame, lambda kind: r.cr[kind].astype(F32)[frame : frame + 1])
    def six(n, carry):
        for row in range(6):
            build(6 * n + row, carry)
        return carry

    lax.fori_loop(0, 12, six, 0)
    lax.fori_loop(0, 18, clear, 0)

    def turn_of(n):
        return jnp.where(n < 3, 3 + n, jnp.where((n < 6) == (f == 0), 6 + n % 3, n % 3))

    def nth(n):
        return n + 3 if n < 3 else n - 3 if n < 6 else n

    def each(low, high, step):
        for n in range(low, high):
            step(n)

    def remote(src, dst, sems, n, to):
        return pltpu.make_async_remote_copy(
            src_ref=src,
            dst_ref=dst,
            send_sem=sems.at[0, n],
            recv_sem=sems.at[1, n],
            device_id=to,
            device_id_type=MESH,
        )

    def swaps(n):
        return [remote(r.kg.at[n, :, pl.ds(1 - core, 1)], r.r0.at[n], r.z, n, partner)]

    def firsts(n):
        b = n % 3
        return [
            remote(
                r.s1.at[n, :, pl.ds((turn(at, b, 0) + k) % 4, 1)],
                r.ra.at[n, k - 1],
                r.y1,
                3 * n + k - 1,
                turned(at, b, 0, k),
            )
            for k in (1, 2, 3)
        ]

    def seconds(n):
        b = n % 3
        return [
            remote(
                r.s2.at[n, :, pl.ds((turn(at, b, 1) + k) % 4, 1)],
                r.rb.at[n, k - 1],
                r.y2,
                3 * n + k - 1,
                turned(at, b, 1, k),
            )
            for k in (1, 2, 3)
        ]

    def thirds(n):
        return [
            remote(r.s3.at[n], r.r3.at[n, k - 1], r.y3, 3 * n + k - 1, turned(at, n % 3, 2, k))
            for k in (1, 2, 3)
        ]

    def start(copies):
        for copy in copies:
            copy.start()

    def weight(n):
        a, b = n // 3, n % 3
        s = jnp.concatenate(
            [r.gs[c, pl.ds(2 - a, 4), pl.ds(2 - b, 16)].reshape(2048, 256) for c in range(3)], 1
        )
        taps = jnp.dot(r.act_t[...], s, preferred_element_type=F32)
        for c in range(3):
            r.kg[n, c] = taps[:, 256 * c : 256 * c + 256].reshape(2, 4, 4, 8, 256)
        start(swaps(n))

    def first(n):
        landed(swaps(n))
        for c in range(3):
            r.s1[n, c] = r.kg[n, c, core] + r.r0[n, c, 0]
        start(firsts(n))

    def second(i):
        n = nth(i)
        landed(firsts(n))
        mine_a = turn(at, n % 3, 0)
        for c in range(3):
            r.s2[n, c] = (r.s1[n, c, mine_a] + r.ra[n, 1, c, 0]) + (
                r.ra[n, 0, c, 0] + r.ra[n, 2, c, 0]
            )
        start(seconds(n))

    def third(i):
        n = nth(i)
        landed(seconds(n))
        mine_b = turn(at, n % 3, 1)
        for c in range(3):
            r.s3[n, c] = (r.s2[n, c, mine_b] + r.rb[n, 1, c, 0]) + (
                r.rb[n, 0, c, 0] + r.rb[n, 2, c, 0]
            )
        start(thirds(n))

    def fourth(i):
        n = nth(i)
        landed(thirds(n))
        a, b = n // 3, n % 3
        r.full[b, core, turn(at, b, 0) * 4 + turn(at, b, 1), a] = (r.s3[n] + r.r3[n, 1]) + (
            r.r3[n, 0] + r.r3[n, 2]
        )

    widest = []
    for p in range(3):
        held = parts[p].at[core, pl.ds(mine[p][2] * 16, 16)]
        widest.append([plan(held, held, along(at, ORDERS[p][2], k)) for k in (1, 2, 3)])

    for p in range(3):
        landed(gather[p])
        start(widest[p])

    def chunk(n, carry):
        @pl.when(n == 6)
        def _():
            landed(face)
            far = [
                jnp.where(f == 0, r.cf[kind].astype(F32)[0:1], r.cf[kind].astype(F32)[3:4])
                for kind in range(4)
            ]
            border(4, lambda kind: far[kind])
            lax.fori_loop(12, 15, six, 0)

        @pl.when(n < 9)
        def _():
            weight(turn_of(n))

        @pl.when(n >= 1)
        def _():
            first(turn_of(n - 1))

        return carry

    lax.fori_loop(0, 10, chunk, 0)
    def align(n, carry):
        x_hi, z, c = n // 8, (n // 2) % 4, n % 2
        for col in range(8):
            spot = {"x": 2 * x_hi + col % 2, "y": col // 2, "z": z}
            for p, (part, (lo, hi)) in enumerate(zip(parts, CUTS)):
                o = ORDERS[p]
                block = part[c, spot[o[2]] * 16 + spot[o[1]] * 4 + spot[o[0]]].astype(F32)
                r.mix[54 * col + lo : 54 * col + hi] = block[: hi - lo]
        r.kal[pl.ds(pl.multiple_of(n * 432, 432), 432), :] = r.mix[...].astype(BF)
        return carry

    def data(q, carry):
        taps = [
            r.gs[t % 3, q + 2 - t // 9, pl.ds(2 - (t // 3) % 3, 16)].reshape(512, 256)
            for t in range(27)
        ]
        sums = jnp.dot(jnp.concatenate(taps, 1), r.kal[...], preferred_element_type=F32)
        r.igv[pl.ds(pl.multiple_of(q * 512, 512), 512), :] = (
            sums / jnp.sqrt(jnp.float32(6912))
        ).astype(BF)
        return carry

    for p in range(3):
        landed(widest[p])
        gather[p] = [go(parts[p].at[core], parts[p].at[core], partner)]
    each(0, 6, second)
    each(0, 3, third)
    each(6, 9, second)
    each(3, 6, third)
    each(0, 3, fourth)
    each(6, 9, third)
    for p in range(3):
        landed(gather[p])
    lax.fori_loop(0, 16, align, 0)
    for n in range(9):
        for copy in swaps(n) + firsts(n):
            copy.wait_send()
    each(3, 9, fourth)

    x = jnp.concatenate(
        [r.full[p, core, mine[p][0] * 4 + mine[p][1]].reshape(72, 256) for p in range(3)], 0
    )
    high, low = halves(x)
    grams = jnp.dot(
        x.T.astype(BF), jnp.concatenate([high, low], 1), preferred_element_type=F32
    )
    gram = 0.25 * (grams[:, :256] + (grams[:, 256:] + grams[:, 256:].T))
    for p, block in enumerate((gram[:128, :128], gram[:128, 128:], gram[128:, 128:])):
        r.gp[p] = block.reshape(2, 64, 128)
    halfgram = go(r.gp.at[:, 1 - core], r.gr0, partner)
    spread = []
    for p in range(3):
        held = r.full.at[p, core, mine[p][0] * 4 + mine[p][1]]
        spread.append(three(lambda k: held, lambda k: held, p, 1))
    sides, relayed = [], []
    for p in range(3):
        axis, home = ORDERS[p][0], mine[p][0] * 4
        before, after = (home + 12) % 16, (home + 4) % 16

        def block(low, count):
            return r.full.at[p, core, pl.ds(low, count)]

        sides.append([plan(block(home, 4), block(home, 4), along(at, axis, k)) for k in (1, 3)])
        relayed.append(
            [
                plan(block(before, 2), block(before, 2), along(at, axis, 1)),
                plan(block(after + 2, 2), block(after + 2, 2), along(at, axis, 3)),
            ]
        )
    landed([halfgram])
    r.ga[0] = r.gp[:, core] + r.gr0[...]

    def sums(n, carry):
        hops = [
            [
                remote(r.ga.at[n, p], r.gr.at[n, p, k - 1], r.y4, 9 * n + 3 * p + k - 1, turned(at, p, n, k))
                for k in (1, 2, 3)
            ]
            for p in range(3)
        ]
        for p in range(3):
            start(hops[p])

        @pl.when(n == AG)
        def _():
            for p in range(3):
                landed(spread[p])
                start(sides[p])

        data(n, 0)
        for p in range(3):
            landed(hops[p])
            r.ga[n + 1, p] = (r.ga[n, p] + r.gr[n, p, 1]) + (r.gr[n, p, 0] + r.gr[n, p, 2])
        for p in range(3):
            for copy in hops[p]:
                copy.wait_send()
        return carry

    lax.fori_loop(0, 3, sums, 0)
    r.gfull[core] = r.ga[3]
    other = go(r.gfull.at[core], r.gfull.at[core], partner)
    data(3, 0)
    keep_ig = keep(r.igv, ig)
    for n in range(9):
        for copy in seconds(n) + thirds(n):
            copy.wait_send()
    landed([other])
    b0, b1, b2 = [r.gfull[:, p].reshape(128, 128) for p in range(3)]
    r.total[...] = jnp.concatenate(
        [jnp.concatenate([b0, b1], 1), jnp.concatenate([b1.T, b2], 1)], 0
    )

    row = lax.broadcasted_iota(jnp.int32, (256, 256), 0)
    column = lax.broadcasted_iota(jnp.int32, (256, 256), 1)
    identity = jnp.where(row == column, 1.0, 0.0).astype(F32)
    factor = r.total[...] + (damping[0, 0] / 256.0) * whole(r.total[...] * identity) * identity
    scale = 2.5 / jnp.sqrt(whole(factor * factor))
    r.root[...] = jnp.sqrt(jnp.sqrt(scale)) * identity
    r.matrix[...] = scale * factor

    def newton(n, carry):
        middle = (5.0 * identity - r.matrix[...]) / 4.0
        r.root[...] = product(r.root[...], middle)
        square = product(middle, middle)
        r.matrix[...] = product(square, product(square, r.matrix[...]))

        @pl.when(n == ON)
        def _():
            for p in range(3):
                landed(sides[p])
                start(relayed[p])

        return carry

    lax.fori_loop(0, ITERS, newton, 0)
    root = r.root[...]
    energy = whole(root * product(r.total[...], root))
    size = jnp.sqrt(energy / (6912.0 * 256.0) + 1e-6)
    rh, rl = halves(root * (0.5 / size))
    stack = jnp.concatenate([rh, rl, rh], 0)

    def page(n):
        return pltpu.make_async_copy(
            r.pages.at[n], out.at[pl.ds(3 * n, 3), core], r.psem.at[n]
        )

    def paired(n):
        return remote(r.pages.at[n], out.at[pl.ds(3 * n, 3), core], r.y5, n, partner)

    def write(n, carry):
        high, low = halves(
            jnp.concatenate(
                [r.full[n % 3, core, :, n // 3, c].reshape(128, 256) for c in range(3)], 0
            )
        )
        direction = jnp.dot(
            jnp.concatenate([high, high, low], 1), stack, preferred_element_type=F32
        )
        for c in range(3):
            rows = pl.ds(pl.multiple_of(768 * n + 256 * c + 128 * core, 128), 128)
            old = r.kal[rows, :].astype(F32)
            r.pages[n, c] = (old - direction[128 * c : 128 * c + 128]).astype(BF)
        paired(n).start()
        page(n).start()
        return carry

    for p in range(3):
        landed(relayed[p])
    lax.fori_loop(0, 9, write, 0)
    for n in range(9):
        page(n).wait()
        paired(n).wait()
    keep_ig.wait()
    for copy in sent:
        copy.wait_send()
    assert len(sent) <= N_SENDS, len(sent)


def step(g, own, act, damping):
    return pl.pallas_call(
        step_kernel,
        out_shape=(VMEM((2048, 256), BF), VMEM((27, 2, 128, 256), BF)),
        in_specs=[pl.BlockSpec(memory_space=pl.ANY)] * 3
        + [pl.BlockSpec(memory_space=pltpu.SMEM)],
        out_specs=[pl.BlockSpec(memory_space=pl.ANY)] * 2,
        scratch_shapes=list(SCRATCH.values()),
        compiler_params=pltpu.CompilerParams(
            collective_id=0, has_side_effects=True, vmem_limit_bytes=LIMIT
        ),
        name="step",
    )(g, own, act, damping)


def on_device(activations, out_grad, kernel, damping):
    ig, new = step(
        out_grad, kernel, activations.reshape(2048, 256), damping.reshape(1, 1)
    )
    return ig.reshape(activations.shape), new.reshape(6912, 256)


def solution(mesh):
    placed = (
        P("frame", "height", "width", None),
        P("frame", "height", "width", None),
        P(("frame", "height", "width"), None),
        P(),
    )
    return jax.shard_map(
        on_device,
        mesh=mesh,
        in_specs=placed,
        out_specs=(P("frame", "height", "width", None), P()),
        check_vma=False,
    )
```

```python
import functools

import jax
import jax.numpy as jnp
from jax import lax
from jax.experimental import pallas as pl
from jax.experimental.pallas import tpu as pltpu
from jax.sharding import PartitionSpec as P

MESH = pl.DeviceIdType.MESH
ITERS = 12
PASS, AG, ON = 8, 2, 5
VMEM = pltpu.VMEM
BF = jnp.bfloat16
F32 = jnp.float32
LIMIT = 51 * 1024 * 1024
ORDERS = (("x", "y", "z"), ("y", "z", "x"), ("z", "x", "y"))
CUTS = ((0, 16), (16, 32), (32, 54))


def place():
    f, h, w = lax.axis_index("frame"), lax.axis_index("height"), lax.axis_index("width")
    return {"x": 2 * f + w % 2, "y": w // 2, "z": h // 2, "c": h % 2}


def device(at):
    return (at["x"] // 2, 2 * at["z"] + at["c"], 2 * at["y"] + at["x"] % 2)


def along(at, axis, k):
    moved = dict(at)
    moved[axis] = (at[axis] + k) % 4
    return device(moved)


def turn(at, b, s):
    which = (b + s) % 3
    if isinstance(which, int):
        return at["xyz"[which]]
    return jnp.where(which == 0, at["x"], jnp.where(which == 1, at["y"], at["z"]))


def turned(at, b, s, k):
    which, moved = (b + s) % 3, dict(at)
    if isinstance(which, int):
        return along(at, "xyz"[which], k)
    for n, axis in enumerate("xyz"):
        moved[axis] = jnp.where(which == n, (at[axis] + k) % 4, at[axis])
    return device(moved)


def other_core(at):
    moved = dict(at)
    moved["c"] = 1 - at["c"]
    return device(moved)


def meet(partners):
    barrier = pltpu.get_barrier_semaphore()
    for partner in partners:
        pl.semaphore_signal(barrier, inc=1, device_id=partner, device_id_type=MESH)
    pl.semaphore_wait(barrier, len(partners))


def halves(x):
    high = x.astype(BF)
    return high, (x - high.astype(F32)).astype(BF)


def product(left, right):
    lh, ll = halves(left)
    rh, rl = halves(right)
    return jnp.dot(
        jnp.concatenate([lh, lh, ll], 1),
        jnp.concatenate([rh, rl, rh], 0),
        preferred_element_type=F32,
    )


def whole(x):
    return jnp.sum(jnp.sum(x, axis=1, keepdims=True), axis=0, keepdims=True)


N_SENDS = 110
SCRATCH = dict(
    gc=VMEM((5, 18, 32, 256), BF),
    act=VMEM((2048, 256), BF),
    ownv=VMEM((54, 256), BF),
    o0=VMEM((16, 256), BF),
    o1=VMEM((16, 256), BF),
    o2=VMEM((24, 256), BF),
    lc=VMEM((5, 16, 256), BF),
    rc=VMEM((5, 16, 256), BF),
    edge=VMEM((2, 4, 16, 256), BF),
    spots=VMEM((4, 16, 256), F32),
    cs=VMEM((4, 16, 256), BF),
    cr=VMEM((4, 16, 256), BF),
    cf=VMEM((4, 16, 256), BF),
    k0=VMEM((2, 64, 16, 256), BF),
    k1=VMEM((2, 64, 16, 256), BF),
    k2=VMEM((2, 64, 24, 256), BF),
    gs=VMEM((3, 6, 18, 32, 256), BF),
    lf=VMEM((5, 18, 256), F32),
    rf=VMEM((5, 18, 256), F32),
    act_t=VMEM((256, 2048), BF),
    mix=VMEM((432, 256), F32),
    kal=VMEM((6912, 256), BF),
    kg=VMEM((9, 3, 2, 4, 4, 8, 256), F32),
    r0=VMEM((9, 3, 1, 4, 4, 8, 256), F32),
    s1=VMEM((9, 3, 4, 4, 8, 256), F32),
    ra=VMEM((9, 3, 3, 1, 4, 8, 256), F32),
    s2=VMEM((9, 3, 4, 8, 256), F32),
    rb=VMEM((9, 3, 3, 1, 8, 256), F32),
    s3=VMEM((9, 3, 8, 256), F32),
    r3=VMEM((9, 3, 3, 8, 256), F32),
    full=VMEM((3, 2, 16, 3, 3, 8, 256), F32),
    pages=VMEM((9, 3, 128, 256), BF),
    psem=pltpu.SemaphoreType.DMA((9,)),
    y5=pltpu.SemaphoreType.DMA((2, 9)),
    z=pltpu.SemaphoreType.DMA((2, 9)),
    y1=pltpu.SemaphoreType.DMA((2, 27)),
    y2=pltpu.SemaphoreType.DMA((2, 27)),
    y3=pltpu.SemaphoreType.DMA((2, 27)),
    gp=VMEM((3, 2, 64, 128), F32),
    gr0=VMEM((3, 64, 128), F32),
    ga=VMEM((4, 3, 64, 128), F32),
    y4=pltpu.SemaphoreType.DMA((2, 27)),
    gr=VMEM((3, 3, 3, 64, 128), F32),
    gfull=VMEM((2, 3, 64, 128), F32),
    total=VMEM((256, 256), F32),
    root=VMEM((256, 256), F32),
    matrix=VMEM((256, 256), F32),
    igv=VMEM((2048, 256), BF),
    sems=pltpu.SemaphoreType.DMA((N_SENDS,)),
    rsems=pltpu.SemaphoreType.DMA((N_SENDS,)),
    lsem=pltpu.SemaphoreType.DMA((16,)),
)


class Refs:
    pass


def step_kernel(g, own, act, damping, ig, out, *scratch):
    r = Refs()
    for name, ref in zip(SCRATCH, scratch):
        setattr(r, name, ref)
    at = place()
    f, h, w = lax.axis_index("frame"), lax.axis_index("height"), lax.axis_index("width")
    hu, hd, wl, wr = (h + 7) % 8, (h + 1) % 8, (w + 7) % 8, (w + 1) % 8
    up, down, left, right = (f, hu, w), (f, hd, w), (f, h, wl), (f, h, wr)
    across = (1 - f, h, w)
    corners = [(f, hd, wr), (f, hd, wl), (f, hu, wr), (f, hu, wl)]
    core = at["c"]
    partner = other_core(at)
    parts = (r.k0, r.k1, r.k2)
    mine = [[at[axis] for axis in o] for o in ORDERS]
    sent, kept = [], []

    def plan(src, dst, to):
        n = len(sent)
        sent.append(
            pltpu.make_async_remote_copy(
                src_ref=src,
                dst_ref=dst,
                send_sem=r.sems.at[n],
                recv_sem=r.rsems.at[n],
                device_id=to,
                device_id_type=MESH,
            )
        )
        return sent[-1]

    def go(src, dst, to):
        copy = plan(src, dst, to)
        copy.start()
        return copy

    def keep(src, dst):
        copy = pltpu.make_async_copy(src, dst, r.lsem.at[len(kept)])
        copy.start()
        kept.append(copy)
        return copy

    def three(src, dst, p, s):
        return [go(src(k), dst(k), along(at, ORDERS[p][s], k)) for k in (1, 2, 3)]

    def landed(copies):
        for copy in copies:
            copy.wait_recv()

    index = [m[2] * 16 + m[1] * 4 + m[0] for m in mine]
    inside = keep(g, r.gc.at[0:4, 1:17])
    flat = keep(act, r.act)
    held_rows = keep(own, r.ownv)
    meet(
        [up, down, left, right, across, partner]
        + corners
        + [along(at, axis, k) for axis in "xyz" for k in (1, 2, 3)]
    )
    last = 3 * (1 - f)
    near = [
        go(g.at[:, 0:1], r.gc.at[0:4, 17:18], up),
        go(g.at[:, 15:16], r.gc.at[0:4, 0:1], down),
    ]
    face = [go(g.at[last], r.gc.at[4, 1:17], across)]
    line = lax.broadcasted_iota(jnp.int32, (32, 512), 0)
    spot = lax.broadcasted_iota(jnp.int32, (32, 512), 1)
    want = jnp.where(line < 16, line * 32 + 31, (line - 16) * 32)
    pick = jnp.where(spot == want, 1.0, 0.0).astype(BF)
    r.spots[...] = jnp.zeros((4, 16, 256), F32)
    held_rows.wait()
    r.o0[...] = r.ownv[0:16, :]
    r.o1[...] = r.ownv[16:32, :]
    r.mix[0:24, :] = jnp.zeros((24, 256), F32)
    r.mix[0:22, :] = r.ownv[32:54, :].astype(F32)
    r.o2[...] = r.mix[0:24, :].astype(BF)
    gather = []
    for p, rows in enumerate((r.o0, r.o1, r.o2)):
        keep(rows, parts[p].at[core, index[p]])
        gather.append(three(lambda k: rows, lambda k: parts[p].at[core, index[p]], p, 0))
    inside.wait()
    for frame in range(4):
        block = r.gc[frame, 1:17].reshape(512, 256)
        cut = jnp.dot(pick, block, preferred_element_type=F32)
        r.edge[0, frame] = cut[:16].astype(BF)
        r.edge[1, frame] = cut[16:].astype(BF)
        for kind, n in enumerate((15, 31, 0, 16)):
            r.spots[kind, frame : frame + 1, :] = cut[n : n + 1]
    r.cs[...] = r.spots[...].astype(BF)
    near += [
        go(r.edge.at[0], r.lc.at[0:4], right),
        go(r.edge.at[1], r.rc.at[0:4], left),
    ] + [go(r.cs.at[kind], r.cr.at[kind], to) for kind, to in enumerate(corners)]
    flat.wait()

    def flip(n, carry):
        rows = pl.ds(pl.multiple_of(256 * n, 256), 256)
        r.act_t[:, rows] = r.act[rows, :].astype(F32).T.astype(BF)
        return carry

    lax.fori_loop(0, 8, flip, 0)
    for copy in kept[3:6]:
        copy.wait()
    for p in range(3):
        landed(gather[p])
        held = parts[p].at[core, pl.ds(mine[p][2] * 16 + mine[p][1] * 4, 4)]
        gather[p] = three(lambda k: held, lambda k: held, p, 1)
    landed(near)
    face += [
        go(r.gc.at[last, 0:1], r.gc.at[4, 0:1], across),
        go(r.gc.at[last, 17:18], r.gc.at[4, 17:18], across),
        go(r.lc.at[last], r.lc.at[4], across),
        go(r.rc.at[last], r.rc.at[4], across),
        go(r.cr, r.cf, across),
    ]

    sub = lax.broadcasted_iota(jnp.int32, (32, 256), 0)

    def build(n, carry):
        frame, row = n // 18, n % 18
        slot = jnp.where(frame == 4, 5 * (1 - f), frame + 1)
        off = jnp.logical_or(
            jnp.logical_and(row == 0, h == 0), jnp.logical_and(row == 17, h == 7)
        )
        keep = jnp.where(off, 0.0, 1.0)
        x = r.gc[frame, row].astype(F32) * keep
        before = r.lf[frame, pl.ds(row, 1), :] * keep
        after = r.rf[frame, pl.ds(row, 1), :] * keep
        r.gs[1, slot, row] = x.astype(BF)
        r.gs[0, slot, row] = jnp.where(sub == 31, after, pltpu.roll(x, 31, 0)).astype(BF)
        r.gs[2, slot, row] = jnp.where(sub == 0, before, pltpu.roll(x, 1, 0)).astype(BF)
        return carry

    def clear(n, carry):
        for c in range(3):
            r.gs[c, 5 * f, n] = jnp.zeros((32, 256), BF)
        return carry

    def border(frame, corner):
        for side, columns, wide, edge in ((0, r.lc, r.lf, 0), (1, r.rc, r.rf, 7)):
            out = w == edge
            wide[frame, 1:17, :] = jnp.where(out, 0.0, columns[frame].astype(F32))
            wide[frame, 0:1, :] = jnp.where(out, 0.0, corner(side))
            wide[frame, 17:18, :] = jnp.where(out, 0.0, corner(2 + side))

    for frame in range(4):
        border(frame, lambda kind: r.cr[kind].astype(F32)[frame : frame + 1])
    def six(n, carry):
        for row in range(6):
            build(6 * n + row, carry)
        return carry

    lax.fori_loop(0, 12, six, 0)
    lax.fori_loop(0, 18, clear, 0)

    def turn_of(n):
        return jnp.where(n < 3, 3 + n, jnp.where((n < 6) == (f == 0), 6 + n % 3, n % 3))

    def nth(n):
        return n + 3 if n < 3 else n - 3 if n < 6 else n

    def each(low, high, step):
        for n in range(low, high):
            step(n)

    def remote(src, dst, sems, n, to):
        return pltpu.make_async_remote_copy(
            src_ref=src,
            dst_ref=dst,
            send_sem=sems.at[0, n],
            recv_sem=sems.at[1, n],
            device_id=to,
            device_id_type=MESH,
        )

    def swaps(n):
        return [remote(r.kg.at[n, :, pl.ds(1 - core, 1)], r.r0.at[n], r.z, n, partner)]

    def firsts(n):
        b = n % 3
        return [
            remote(
                r.s1.at[n, :, pl.ds((turn(at, b, 0) + k) % 4, 1)],
                r.ra.at[n, k - 1],
                r.y1,
                3 * n + k - 1,
                turned(at, b, 0, k),
            )
            for k in (1, 2, 3)
        ]

    def seconds(n):
        b = n % 3
        return [
            remote(
                r.s2.at[n, :, pl.ds((turn(at, b, 1) + k) % 4, 1)],
                r.rb.at[n, k - 1],
                r.y2,
                3 * n + k - 1,
                turned(at, b, 1, k),
            )
            for k in (1, 2, 3)
        ]

    def thirds(n):
        return [
            remote(r.s3.at[n], r.r3.at[n, k - 1], r.y3, 3 * n + k - 1, turned(at, n % 3, 2, k))
            for k in (1, 2, 3)
        ]

    def start(copies):
        for copy in copies:
            copy.start()

    def weight(n):
        a, b = n // 3, n % 3
        s = jnp.concatenate(
            [r.gs[c, pl.ds(2 - a, 4), pl.ds(2 - b, 16)].reshape(2048, 256) for c in range(3)], 1
        )
        taps = jnp.dot(r.act_t[...], s, preferred_element_type=F32)
        for c in range(3):
            r.kg[n, c] = taps[:, 256 * c : 256 * c + 256].reshape(2, 4, 4, 8, 256)
        start(swaps(n))

    def first(n):
        landed(swaps(n))
        for c in range(3):
            r.s1[n, c] = r.kg[n, c, core] + r.r0[n, c, 0]
        start(firsts(n))

    def second(i):
        n = nth(i)
        landed(firsts(n))
        mine_a = turn(at, n % 3, 0)
        for c in range(3):
            r.s2[n, c] = (r.s1[n, c, mine_a] + r.ra[n, 1, c, 0]) + (
                r.ra[n, 0, c, 0] + r.ra[n, 2, c, 0]
            )
        start(seconds(n))

    def third(i):
        n = nth(i)
        landed(seconds(n))
        mine_b = turn(at, n % 3, 1)
        for c in range(3):
            r.s3[n, c] = (r.s2[n, c, mine_b] + r.rb[n, 1, c, 0]) + (
                r.rb[n, 0, c, 0] + r.rb[n, 2, c, 0]
            )
        start(thirds(n))

    def fourth(i):
        n = nth(i)
        landed(thirds(n))
        a, b = n // 3, n % 3
        r.full[b, core, turn(at, b, 0) * 4 + turn(at, b, 1), a] = (r.s3[n] + r.r3[n, 1]) + (
            r.r3[n, 0] + r.r3[n, 2]
        )

    widest, onward = [], []
    for p in range(3):
        axis, home = ORDERS[p][2], mine[p][2] * 16
        before, after = (home + 48) % 64, (home + 16) % 64

        def slots(low, count):
            return parts[p].at[core, pl.ds(low, count)]

        widest.append([plan(slots(home, 16), slots(home, 16), along(at, axis, k)) for k in (1, 3)])
        onward.append(
            [
                plan(slots(before, 8), slots(before, 8), along(at, axis, 1)),
                plan(slots(after + 8, 8), slots(after + 8, 8), along(at, axis, 3)),
            ]
        )

    for p in range(3):
        landed(gather[p])
        start(widest[p])

    def chunk(n, carry):
        @pl.when(n == PASS)
        def _():
            for p in range(3):
                landed(widest[p])
                start(onward[p])

        @pl.when(n == 6)
        def _():
            landed(face)
            far = [
                jnp.where(f == 0, r.cf[kind].astype(F32)[0:1], r.cf[kind].astype(F32)[3:4])
                for kind in range(4)
            ]
            border(4, lambda kind: far[kind])
            lax.fori_loop(12, 15, six, 0)

        @pl.when(n < 9)
        def _():
            weight(turn_of(n))

        @pl.when(n >= 1)
        def _():
            first(turn_of(n - 1))

        return carry

    lax.fori_loop(0, 10, chunk, 0)
    def align(n, carry):
        x_hi, z, c = n // 8, (n // 2) % 4, n % 2
        for col in range(8):
            spot = {"x": 2 * x_hi + col % 2, "y": col // 2, "z": z}
            for p, (part, (lo, hi)) in enumerate(zip(parts, CUTS)):
                o = ORDERS[p]
                block = part[c, spot[o[2]] * 16 + spot[o[1]] * 4 + spot[o[0]]].astype(F32)
                r.mix[54 * col + lo : 54 * col + hi] = block[: hi - lo]
        r.kal[pl.ds(pl.multiple_of(n * 432, 432), 432), :] = r.mix[...].astype(BF)
        return carry

    def data(q, carry):
        taps = [
            r.gs[t % 3, q + 2 - t // 9, pl.ds(2 - (t // 3) % 3, 16)].reshape(512, 256)
            for t in range(27)
        ]
        sums = jnp.dot(jnp.concatenate(taps, 1), r.kal[...], preferred_element_type=F32)
        r.igv[pl.ds(pl.multiple_of(q * 512, 512), 512), :] = (
            sums / jnp.sqrt(jnp.float32(6912))
        ).astype(BF)
        return carry

    for p in range(3):
        landed(onward[p])
        gather[p] = [go(parts[p].at[core], parts[p].at[core], partner)]
    each(0, 6, second)
    each(0, 3, third)
    each(6, 9, second)
    each(3, 6, third)
    each(0, 3, fourth)
    each(6, 9, third)
    for p in range(3):
        landed(gather[p])
    lax.fori_loop(0, 16, align, 0)
    for n in range(9):
        for copy in swaps(n) + firsts(n):
            copy.wait_send()
    each(3, 9, fourth)

    x = jnp.concatenate(
        [r.full[p, core, mine[p][0] * 4 + mine[p][1]].reshape(72, 256) for p in range(3)], 0
    )
    high, low = halves(x)
    grams = jnp.dot(
        x.T.astype(BF), jnp.concatenate([high, low], 1), preferred_element_type=F32
    )
    gram = 0.25 * (grams[:, :256] + (grams[:, 256:] + grams[:, 256:].T))
    for p, block in enumerate((gram[:128, :128], gram[:128, 128:], gram[128:, 128:])):
        r.gp[p] = block.reshape(2, 64, 128)
    halfgram = go(r.gp.at[:, 1 - core], r.gr0, partner)
    spread = []
    for p in range(3):
        held = r.full.at[p, core, mine[p][0] * 4 + mine[p][1]]
        spread.append(three(lambda k: held, lambda k: held, p, 1))
    sides, relayed = [], []
    for p in range(3):
        axis, home = ORDERS[p][0], mine[p][0] * 4
        before, after = (home + 12) % 16, (home + 4) % 16

        def block(low, count):
            return r.full.at[p, core, pl.ds(low, count)]

        sides.append([plan(block(home, 4), block(home, 4), along(at, axis, k)) for k in (1, 3)])
        relayed.append(
            [
                plan(block(before, 2), block(before, 2), along(at, axis, 1)),
                plan(block(after + 2, 2), block(after + 2, 2), along(at, axis, 3)),
            ]
        )
    landed([halfgram])
    r.ga[0] = r.gp[:, core] + r.gr0[...]

    def sums(n, carry):
        hops = [
            [
                remote(r.ga.at[n, p], r.gr.at[n, p, k - 1], r.y4, 9 * n + 3 * p + k - 1, turned(at, p, n, k))
                for k in (1, 2, 3)
            ]
            for p in range(3)
        ]
        for p in range(3):
            start(hops[p])

        @pl.when(n == AG)
        def _():
            for p in range(3):
                landed(spread[p])
                start(sides[p])

        data(n, 0)
        for p in range(3):
            landed(hops[p])
            r.ga[n + 1, p] = (r.ga[n, p] + r.gr[n, p, 1]) + (r.gr[n, p, 0] + r.gr[n, p, 2])
        for p in range(3):
            for copy in hops[p]:
                copy.wait_send()
        return carry

    lax.fori_loop(0, 3, sums, 0)
    r.gfull[core] = r.ga[3]
    other = go(r.gfull.at[core], r.gfull.at[core], partner)
    data(3, 0)
    keep_ig = keep(r.igv, ig)
    for n in range(9):
        for copy in seconds(n) + thirds(n):
            copy.wait_send()
    landed([other])
    b0, b1, b2 = [r.gfull[:, p].reshape(128, 128) for p in range(3)]
    r.total[...] = jnp.concatenate(
        [jnp.concatenate([b0, b1], 1), jnp.concatenate([b1.T, b2], 1)], 0
    )

    row = lax.broadcasted_iota(jnp.int32, (256, 256), 0)
    column = lax.broadcasted_iota(jnp.int32, (256, 256), 1)
    identity = jnp.where(row == column, 1.0, 0.0).astype(F32)
    factor = r.total[...] + (damping[0, 0] / 256.0) * whole(r.total[...] * identity) * identity
    scale = 2.5 / jnp.sqrt(whole(factor * factor))
    r.root[...] = jnp.sqrt(jnp.sqrt(scale)) * identity
    r.matrix[...] = scale * factor

    def newton(n, carry):
        middle = (5.0 * identity - r.matrix[...]) / 4.0
        r.root[...] = product(r.root[...], middle)
        square = product(middle, middle)
        r.matrix[...] = product(square, product(square, r.matrix[...]))

        @pl.when(n == ON)
        def _():
            for p in range(3):
                landed(sides[p])
                start(relayed[p])

        return carry

    lax.fori_loop(0, ITERS, newton, 0)
    root = r.root[...]
    energy = whole(root * product(r.total[...], root))
    size = jnp.sqrt(energy / (6912.0 * 256.0) + 1e-6)
    rh, rl = halves(root * (0.5 / size))
    stack = jnp.concatenate([rh, rl, rh], 0)

    def page(n):
        return pltpu.make_async_copy(
            r.pages.at[n], out.at[pl.ds(3 * n, 3), core], r.psem.at[n]
        )

    def paired(n):
        return remote(r.pages.at[n], out.at[pl.ds(3 * n, 3), core], r.y5, n, partner)

    def write(n, carry):
        high, low = halves(
            jnp.concatenate(
                [r.full[n % 3, core, :, n // 3, c].reshape(128, 256) for c in range(3)], 0
            )
        )
        direction = jnp.dot(
            jnp.concatenate([high, high, low], 1), stack, preferred_element_type=F32
        )
        for c in range(3):
            rows = pl.ds(pl.multiple_of(768 * n + 256 * c + 128 * core, 128), 128)
            old = r.kal[rows, :].astype(F32)
            r.pages[n, c] = (old - direction[128 * c : 128 * c + 128]).astype(BF)
        paired(n).start()
        page(n).start()
        return carry

    for p in range(3):
        landed(relayed[p])
    lax.fori_loop(0, 9, write, 0)
    for n in range(9):
        page(n).wait()
        paired(n).wait()
    keep_ig.wait()
    for copy in sent:
        copy.wait_send()
    assert len(sent) <= N_SENDS, len(sent)


def step(g, own, act, damping):
    return pl.pallas_call(
        step_kernel,
        out_shape=(VMEM((2048, 256), BF), VMEM((27, 2, 128, 256), BF)),
        in_specs=[pl.BlockSpec(memory_space=pl.ANY)] * 3
        + [pl.BlockSpec(memory_space=pltpu.SMEM)],
        out_specs=[pl.BlockSpec(memory_space=pl.ANY)] * 2,
        scratch_shapes=list(SCRATCH.values()),
        compiler_params=pltpu.CompilerParams(
            collective_id=0, has_side_effects=True, vmem_limit_bytes=LIMIT
        ),
        name="step",
    )(g, own, act, damping)


def on_device(activations, out_grad, kernel, damping):
    ig, new = step(
        out_grad, kernel, activations.reshape(2048, 256), damping.reshape(1, 1)
    )
    return ig.reshape(activations.shape), new.reshape(6912, 256)


def solution(mesh):
    placed = (
        P("frame", "height", "width", None),
        P("frame", "height", "width", None),
        P(("frame", "height", "width"), None),
        P(),
    )
    return jax.shard_map(
        on_device,
        mesh=mesh,
        in_specs=placed,
        out_specs=(P("frame", "height", "width", None), P()),
        check_vma=False,
    )
```
